32 devices in a mesh: freq: 4 (over x, core), rcv: 8 (over z, y).
Axes of the slice: x: 2, y: 2, z: 4, core: 2. Of those that a mesh axis runs over, the one named last changes fastest.
Arguments:
- reflection: bfloat16 [8, 2, 2560, 2560], P('freq', None, 'rcv'), may hold values from -5 to 5, as said below
- starts: int32 [2560, 192], P('rcv'), may hold values from 8 to 56
- focusing: float32 [8, 2560, 2, 192], P('freq', 'rcv'), may hold values from -6 to 6
- residual: float32 [8, 2560, 2, 192], P('freq', 'rcv'), may hold values from -6 to 6
- direction: float32 [8, 2560, 2, 192], P('freq', 'rcv'), may hold values from -6 to 6
- gradient: float32 [8, 2560, 2, 192], P('freq', 'rcv'), may hold values from -30 to 30
Outputs:
- new_focusing: float32 [8, 2560, 2, 192], P('freq', 'rcv')
- new_residual: float32 [8, 2560, 2, 192], P('freq', 'rcv')
- new_direction: float32 [8, 2560, 2, 192], P('freq', 'rcv')
- green_field: float32 [8, 2560, 2, 192], P('freq', 'rcv')
- focal_correlation: float32 [8, 2, 192], P('freq')
The draws below stay inside these ranges and needn't reach their ends.
Inputs may be any that keep to these rules, and one draw needn't show every extreme that they name: Each frequency's matrix is symmetric in source and receiver: reflection[f, c, s, r] = reflection[f, c, r, s].
All inputs are finite; a program needn't handle non-finite values.
Results may differ from the reference program's by a relative error of at most 0.0003.
The reference program's roundings to bfloat16 on the way (of `gated`) count: a program that leaves them out, or rounds other values in their place, can miss the bound.
Values may be sent and summed in bfloat16 or wider, within the bound.
No kernel may reach another device: no remote copies, remote signals or barrier semaphores. Data moves between devices by JAX's collectives and lax.ppermute only.
A program may use at most 64 MiB of HBM per device.

```python
import math
import jax
import jax.numpy as jnp
from jax import lax

N = 2560
K = 192
F = 8
TS = 64


def rising(count):
    position = jnp.arange(count, dtype=jnp.float32)
    return 3.0 ** (position / max(count - 1, 1) - 0.5)


def draw_reflection(key, part):
    row_scale = rising(N)
    freq_scale = rising(F)

    def single(position):
        noise = jnp.clip(jax.random.normal(jax.random.fold_in(key, position), (2, N, N), jnp.float32), -6.0, 6.0)
        symmetric = (noise + jnp.transpose(noise, (0, 2, 1))) * (0.5 / math.sqrt(N))
        scaled = symmetric * row_scale[:, None] * row_scale[None, :] * freq_scale[position]
        return scaled.astype(jnp.bfloat16)
    return lax.map(single, jnp.arange(F, dtype=jnp.int32))


def draw_gradient(key, part):
    noise = jnp.clip(jax.random.normal(key, (F, N, 2, K), jnp.float32), -6.0, 6.0) * 0.5
    row_scale = rising(N)
    scale = rising(F)[:, None, None, None] * row_scale[None, :, None, None]
    return noise * scale


def with_ends(values, rng, low, high):
    longest = values.shape.index(max(values.shape))
    spots = []
    for shift in (0, 1):
        where = [jax.random.randint(jax.random.fold_in(rng, axis), (), 0, length) for axis, length in enumerate(values.shape)]
        where[longest] = (where[longest] + shift) % values.shape[longest]
        spots.append(tuple(where))
    return values.at[spots[0]].set(low).at[spots[1]].set(high)


def levels(stream_key, extent, split, least, largest):
    loudness = 1.0
    for dim, shards_of in split:
        draws = jax.random.uniform(jax.random.fold_in(jax.random.fold_in(stream_key, 6), dim), (shards_of,), jnp.float32, least / len(split), largest / len(split))
        loudness = loudness * jnp.repeat(jnp.exp(draws), extent[dim] // shards_of).reshape((-1,) + (1,) * (len(extent) - 1 - dim))
    return loudness


def normal_values(key, extent, width, bound, shards=(), held_as=jnp.bfloat16):
    result = width * jax.random.normal(key, extent, jnp.float32)
    if shards:
        result = result * levels(key, extent, shards, -0.22, 0.18)
    return jnp.clip(result, -bound, bound).astype(held_as)


def setup_inputs(seed: int = 0) -> dict:
    splits = jax.random.split(jax.random.key(seed), 7)
    return {
        "reflection": draw_reflection(jax.random.fold_in(splits[6], 71), 0),
        "starts": with_ends(jax.random.randint(splits[1], (N, K), TS // 8, TS - TS // 8 + 1), jax.random.fold_in(splits[1], 1), TS // 8, (TS - TS // 8 + 1) - 1).astype(jnp.int32),
        "focusing": normal_values(splits[2], (F, N, 2, K), 1.0, 6.0, ((0, 4), (1, 8)), jnp.float32),
        "residual": normal_values(splits[3], (F, N, 2, K), 1.0, 6.0, ((0, 4), (1, 8)), jnp.float32),
        "direction": normal_values(splits[4], (F, N, 2, K), 1.0, 6.0, ((0, 4), (1, 8)), jnp.float32),
        "gradient": draw_gradient(jax.random.fold_in(splits[6], 71), 0),
    }


band_start = 5
tiny = 1e-06
highest = lax.Precision.HIGHEST

def tables(count, offset):
    times = jnp.arange(TS, dtype=jnp.float32)[:, None]
    bins = (jnp.arange(count, dtype=jnp.int32) + offset + band_start).astype(jnp.float32)[None, :]
    phase = 2.0 * jnp.pi * times * bins / TS
    return (jnp.cos(phase), jnp.sin(phase))

def contract_time(table, values):
    return jnp.einsum('tf,frk->trk', table, values, precision=highest)

def contract_back(table, values):
    return jnp.einsum('tf,trk->frk', table, values, precision=highest)

def time_gate(field, forward_cos, forward_sin, back_cos, back_sin, limits, complement):
    real_part = field[:, :, 0]
    imag_part = field[:, :, 1]
    time_real = contract_time(forward_cos, real_part) - contract_time(forward_sin, imag_part)
    time_imag = contract_time(forward_sin, real_part) + contract_time(forward_cos, imag_part)
    clock = jnp.arange(TS, dtype=jnp.int32)[:, None, None]
    window = (clock < limits[None]).astype(jnp.float32)
    if complement:
        window = 1.0 - window
    kept_real = window * time_real
    kept_imag = window * time_imag
    out_real = (contract_back(back_cos, kept_real) + contract_back(back_sin, kept_imag)) / TS
    out_imag = (contract_back(back_cos, kept_imag) - contract_back(back_sin, kept_real)) / TS
    return jnp.stack([out_real, out_imag], axis=2)

def product(left, right):
    return jnp.dot(left, right, preferred_element_type=jnp.float32)

def forward_apply(reflection, values):

    def single(pair):
        matrix, vector = pair
        out_real = product(matrix[0], vector[:, 0]) - product(matrix[1], vector[:, 1])
        out_imag = product(matrix[0], vector[:, 1]) + product(matrix[1], vector[:, 0])
        return jnp.stack([out_real, out_imag], axis=1)
    return lax.map(single, (reflection, values))

def adjoint_apply(reflection, values):

    def single(pair):
        matrix, vector = pair
        real_t = matrix[0].T
        imag_t = matrix[1].T
        out_real = product(real_t, vector[:, 0]) + product(imag_t, vector[:, 1])
        out_imag = product(real_t, vector[:, 1]) - product(imag_t, vector[:, 0])
        return jnp.stack([out_real, out_imag], axis=1)
    return lax.map(single, (reflection, values))

def reference(reflection, starts, focusing, residual, direction, gradient):
    cos_table, sin_table = tables(F, 0)

    def gate(field, complement):
        return time_gate(field, cos_table, sin_table, cos_table, sin_table, starts, complement)
    direction_image = forward_apply(reflection, direction.astype(jnp.bfloat16))
    focusing_image = forward_apply(reflection, focusing.astype(jnp.bfloat16))
    image = gate(direction_image, False)
    gamma = jnp.sum(gradient * gradient)
    curvature = jnp.sum(image * image)
    alpha = gamma / (curvature + tiny)
    new_focusing = focusing + alpha * direction
    new_residual = residual - alpha * image
    gated = gate(new_residual, False).astype(jnp.bfloat16)
    new_gradient = adjoint_apply(reflection, gated)
    new_gamma = jnp.sum(new_gradient * new_gradient)
    new_direction = new_gradient + new_gamma / (gamma + tiny) * direction
    green_field = gate(focusing_image + alpha * direction_image, True)
    corr_real = lax.optimization_barrier(jnp.sum(green_field[:, :, 0] * new_focusing[:, :, 0] + green_field[:, :, 1] * new_focusing[:, :, 1], axis=1))
    corr_imag = lax.optimization_barrier(jnp.sum(green_field[:, :, 1] * new_focusing[:, :, 0] - green_field[:, :, 0] * new_focusing[:, :, 1], axis=1))
    focal_correlation = jnp.stack([corr_real, corr_imag], axis=1) / math.sqrt(N)
    return (new_focusing, new_residual, new_direction, green_field, focal_correlation)
```

```python
import math

import jax
import jax.numpy as jnp
from jax import lax
from jax.experimental import pallas as pl
from jax.experimental.pallas import tpu as pltpu
from jax.sharding import PartitionSpec as P

TS = 64
band_start = 5
tiny = 1e-06
highest = lax.Precision.HIGHEST
LANES = 128
HALF = 64


VMEM = pl.BlockSpec(memory_space=pltpu.VMEM)
SMEM = pl.BlockSpec(memory_space=pltpu.SMEM)
ANY = pl.BlockSpec(memory_space=pl.ANY)


def tables(count):
    times = jnp.arange(TS, dtype=jnp.float32)[:, None]
    bins = (jnp.arange(count, dtype=jnp.int32) + band_start).astype(jnp.float32)[None, :]
    phase = 2.0 * jnp.pi * times * bins / TS
    return (jnp.cos(phase), jnp.sin(phase))


def contract_time(table, values):
    return jnp.einsum("tf,frk->trk", table, values, precision=highest)


def contract_back(table, values):
    return jnp.einsum("tf,trk->frk", table, values, precision=highest)


def time_gate(field, cos_table, sin_table, limits, complement):
    real_part = field[:, :, 0]
    imag_part = field[:, :, 1]
    time_real = contract_time(cos_table, real_part) - contract_time(sin_table, imag_part)
    time_imag = contract_time(sin_table, real_part) + contract_time(cos_table, imag_part)
    clock = jnp.arange(TS, dtype=jnp.int32)[:, None, None]
    window = (clock < limits[None]).astype(jnp.float32)
    if complement:
        window = 1.0 - window
    kept_real = window * time_real
    kept_imag = window * time_imag
    out_real = (contract_back(cos_table, kept_real) + contract_back(sin_table, kept_imag)) / TS
    out_imag = (contract_back(cos_table, kept_imag) - contract_back(sin_table, kept_real)) / TS
    return jnp.stack([out_real, out_imag], axis=2)


def combine(total, conjugate):
    if conjugate:
        out_real = total[:, 0, :, 0] + total[:, 1, :, 1]
        out_imag = total[:, 0, :, 1] - total[:, 1, :, 0]
    else:
        out_real = total[:, 0, :, 0] - total[:, 1, :, 1]
        out_imag = total[:, 0, :, 1] + total[:, 1, :, 0]
    return jnp.stack([out_real, out_imag], axis=2)


def per_device_general(reflection, starts, focusing, residual, direction, gradient):
    local_rows = reflection.shape[2]
    positions = reflection.shape[3]
    groups = lax.axis_size("freq")
    position = lax.axis_index("freq")
    cos_table, sin_table = tables(reflection.shape[0] * groups)

    def gate(field, complement):
        spread = lax.all_to_all(field, "freq", split_axis=1, concat_axis=0, tiled=True)
        share = local_rows // groups
        limits = lax.dynamic_slice_in_dim(starts, position * share, share, 0)
        gated_part = time_gate(spread, cos_table, sin_table, limits, complement)
        return lax.all_to_all(gated_part, "freq", split_axis=0, concat_axis=1, tiled=True)

    def accumulate(piece):
        return jnp.einsum("fpnm,fmqk->fpnqk", reflection, piece, preferred_element_type=jnp.float32)

    direction_low = direction.astype(jnp.bfloat16)
    focusing_low = focusing.astype(jnp.bfloat16)
    aimed_total = accumulate(lax.all_gather(direction_low, "rcv", axis=1, tiled=True))
    direction_image = combine(aimed_total, False)
    gamma = lax.psum(jnp.sum(gradient * gradient), ("freq", "rcv"))
    image = gate(direction_image, False)
    curvature = lax.psum(jnp.sum(image * image), ("freq", "rcv"))
    alpha = gamma / (curvature + tiny)
    new_focusing = focusing + alpha * direction
    new_residual = residual - alpha * image
    gated = gate(new_residual, False).astype(jnp.bfloat16)
    total = accumulate(lax.all_gather(gated, "rcv", axis=1, tiled=True))
    new_gradient = combine(total, True)
    new_gamma = lax.psum(jnp.sum(new_gradient * new_gradient), ("freq", "rcv"))
    new_direction = new_gradient + new_gamma / (gamma + tiny) * direction
    focus_total = accumulate(lax.all_gather(focusing_low, "rcv", axis=1, tiled=True))
    focusing_image = combine(focus_total, False)
    green_field = gate(focusing_image + alpha * direction_image, True)
    corr_real = jnp.sum(
        green_field[:, :, 0] * new_focusing[:, :, 0] + green_field[:, :, 1] * new_focusing[:, :, 1],
        axis=1,
    )
    corr_imag = jnp.sum(
        green_field[:, :, 1] * new_focusing[:, :, 0] - green_field[:, :, 0] * new_focusing[:, :, 1],
        axis=1,
    )
    partial_corr = jnp.stack([corr_real, corr_imag], axis=1)
    focal_correlation = lax.psum(partial_corr, "rcv") / math.sqrt(positions)
    return (new_focusing, new_residual, new_direction, green_field, focal_correlation)


def pack(real, imag):
    main = real.shape[-1] - HALF
    tail = jnp.concatenate([real[:, main:], imag[:, main:]], axis=1)
    return jnp.concatenate([real[:, :main], imag[:, :main], tail], axis=1)


def unpack(row, plane):
    main = row.shape[-1] // 2 - HALF
    tail = 2 * main + plane * HALF
    return row[:, plane * main : (plane + 1) * main], row[:, tail : tail + HALF]


def cost(flops, size):
    return pl.CostEstimate(flops=int(flops), bytes_accessed=int(size), transcendentals=0)


def prep_low_kernel(x_ref, o_ref):
    for f in range(x_ref.shape[0]):
        o_ref[f] = pack(x_ref[f, 0], x_ref[f, 1]).astype(jnp.bfloat16)


def prep_low(x):
    loc, _, k, n = x.shape
    return pl.pallas_call(
        prep_low_kernel,
        out_shape=jax.ShapeDtypeStruct((loc, k, 2 * n), jnp.bfloat16),
        in_specs=[VMEM],
        out_specs=VMEM,
        cost_estimate=cost(x.size, 6 * x.size),
        name="prep_low",
    )(x)


def share_of(me, p, groups):
    if groups & (groups - 1) == 0:
        return me ^ p
    return lax.rem(p - me + groups, groups)


def prep_shares_kernel(groups, pos_ref, x_ref, g_ref, *o_refs):
    me = pos_ref[0]
    ks = x_ref.shape[2] // groups
    for p in range(groups):
        at = pl.multiple_of(share_of(me, p, groups) * ks, ks)
        for f in range(x_ref.shape[0]):
            o_refs[p][f] = pack(x_ref[f, 0, pl.ds(at, ks), :], x_ref[f, 1, pl.ds(at, ks), :])
    total = jnp.zeros((8, g_ref.shape[3]), jnp.float32)
    for f in range(g_ref.shape[0]):
        for c in range(2):
            for r in range(0, g_ref.shape[2], 8):
                v = g_ref[f, c, r : r + 8, :]
                total = total + v * v
    o_refs[groups][...] = lane_fold(jnp.sum(total, axis=0, keepdims=True))


def lane_fold(row):
    out = jnp.sum(row, axis=1, keepdims=True)
    lane = lax.broadcasted_iota(jnp.int32, (1, LANES), 1)
    return jnp.where(lane == 0, out, 0.0)


def prep_shares(pos, x, g, groups):
    loc, _, k, n = x.shape
    outs = [jax.ShapeDtypeStruct((loc, k // groups, 2 * n), jnp.float32)] * groups
    return pl.pallas_call(
        lambda *refs: prep_shares_kernel(groups, *refs),
        out_shape=outs + [jax.ShapeDtypeStruct((1, LANES), jnp.float32)],
        in_specs=[SMEM, VMEM, VMEM],
        out_specs=[VMEM] * (groups + 1),
        cost_estimate=cost(3 * x.size, 12 * x.size),
        name="prep_shares",
    )(pos, x, g)


def product_kernel(groups, tiles, conjugate, shares, pos_ref, r_ref, *refs):
    blocks = refs[:tiles]
    rest = refs[tiles:]
    count = groups if shares else 1
    outs = rest[:count]
    rest = rest[count:]
    if not shares:
        sum_ref, rest = rest[0], rest[1:]
    v_scr, acc_p, acc_q = rest
    f = pl.program_id(0)
    step = pl.program_id(1)
    loc, kc, wide = blocks[0].shape
    n = wide // 2
    depth = r_ref.shape[3]

    @pl.when((f == 0) & (step == 0))
    def _():
        odd = pos_ref[1]
        for b in range(tiles // 2):
            at = pl.multiple_of(pos_ref[2 + b] * wide, LANES)
            for flip in range(2):

                @pl.when(odd == flip)
                def _():
                    even = blocks[2 * b + flip]
                    other = blocks[2 * b + 1 - flip]
                    for g in range(loc):
                        for c in range(2):
                            e_main, e_tail = unpack(even[g], c)
                            o_main, o_tail = unpack(other[g], c)
                            v_scr[g, c * kc : (c + 1) * kc, pl.ds(at, wide)] = jnp.concatenate(
                                [e_main, e_tail, o_main, o_tail], axis=1
                            )

    here = v_scr[f, :, pl.ds(pl.multiple_of(step * depth, depth), depth)]
    dims = (((1,), (1,)), ((), ()))
    p_part = lax.dot_general(here, r_ref[0, 0], dims, preferred_element_type=jnp.float32)
    q_part = lax.dot_general(here, r_ref[0, 1], dims, preferred_element_type=jnp.float32)

    @pl.when(step == 0)
    def _():
        acc_p[...] = p_part
        acc_q[...] = q_part

    @pl.when(step > 0)
    def _():
        acc_p[...] += p_part
        acc_q[...] += q_part

    @pl.when(step == pl.num_programs(1) - 1)
    def _():
        if shares:
            me = pos_ref[0]
            ks = kc // groups
            for p in range(groups):
                at = pl.multiple_of(share_of(me, p, groups) * ks, ks)
                real = acc_p[pl.ds(at, ks), :] - acc_q[pl.ds(at + kc, ks), :]
                imag = acc_p[pl.ds(at + kc, ks), :] + acc_q[pl.ds(at, ks), :]
                outs[p][0] = pack(real, imag)
        else:
            real = acc_p[0:kc, :] + acc_q[kc:, :]
            imag = acc_p[kc:, :] - acc_q[0:kc, :]
            outs[0][0, 0] = real
            outs[0][0, 1] = imag
            part = lane_fold(jnp.sum(real * real + imag * imag, axis=0, keepdims=True))

            @pl.when(f == 0)
            def _():
                sum_ref[...] = part

            @pl.when(f > 0)
            def _():
                sum_ref[...] += part


def product(pos, reflection, blocks, groups, conjugate):
    loc, _, rows, cols = reflection.shape
    kc, wide = blocks[0].shape[1:]
    steps = 5 if cols % (5 * LANES) == 0 else 1
    depth = cols // steps
    shares = not conjugate
    if shares:
        ks = kc // groups
        out_shape = [jax.ShapeDtypeStruct((loc, ks, wide), jnp.float32)] * groups
        out_specs = [pl.BlockSpec((1, ks, wide), lambda f, s: (f, 0, 0))] * groups
    else:
        out_shape = [
            jax.ShapeDtypeStruct((loc, 2, kc, rows), jnp.float32),
            jax.ShapeDtypeStruct((1, LANES), jnp.float32),
        ]
        out_specs = [
            pl.BlockSpec((1, 2, kc, rows), lambda f, s: (f, 0, 0, 0)),
            pl.BlockSpec((1, LANES), lambda f, s: (0, 0)),
        ]
    return pl.pallas_call(
        lambda *refs: product_kernel(groups, len(blocks), conjugate, shares, *refs),
        grid=(loc, steps),
        out_shape=out_shape,
        in_specs=[SMEM, pl.BlockSpec((1, 2, rows, depth), lambda f, s: (f, 0, 0, s))]
        + [VMEM] * len(blocks),
        out_specs=out_specs,
        scratch_shapes=[
            pltpu.VMEM((loc, 2 * kc, cols), jnp.bfloat16),
            pltpu.VMEM((2 * kc, rows), jnp.float32),
            pltpu.VMEM((2 * kc, rows), jnp.float32),
        ],
        cost_estimate=cost(8 * loc * rows * cols * kc, 2 * reflection.size + 4 * loc * cols * kc),
        compiler_params=pltpu.CompilerParams(dimension_semantics=("arbitrary", "arbitrary")),
        name="product_back" if conjugate else "product",
    )(pos, reflection, *blocks)


def gate_weights(limit, count):
    angle = limit * (2.0 * math.pi / TS)
    c1 = jnp.cos(angle)
    s1 = jnp.sin(angle)
    real = [limit * (1.0 / TS)]
    imag = [None]
    c, s = c1, s1
    for d in range(1, count):
        half_cot = 0.5 / math.tan(math.pi * d / TS)
        rest = 1.0 - c
        real.append((0.5 * rest + half_cot * s) * (1.0 / TS))
        imag.append((half_cot * rest - 0.5 * s) * (1.0 / TS))
        c, s = c * c1 - s * s1, s * c1 + c * s1
    return real, imag


def gate_pair(real, imag, ur, ui):
    count = len(ur)
    out_r, out_i = [], []
    for j in range(count):
        r = real[0] * ur[j]
        i = real[0] * ui[j]
        for m in range(count):
            d = abs(m - j)
            if m > j:
                r = r + real[d] * ur[m] - imag[d] * ui[m]
                i = i + real[d] * ui[m] + imag[d] * ur[m]
            elif m < j:
                r = r + real[d] * ur[m] + imag[d] * ui[m]
                i = i + real[d] * ui[m] - imag[d] * ur[m]
        out_r.append(r)
        out_i.append(i)
    return out_r, out_i


def gate_tail(real, signed, u):
    count = len(u)
    w = [pltpu.roll(v, HALF, 1) for v in u]
    outs = []
    for j in range(count):
        r = real[0] * u[j]
        for m in range(count):
            d = abs(m - j)
            if m > j:
                r = r + real[d] * u[m] + signed[d] * w[m]
            elif m < j:
                r = r + real[d] * u[m] - signed[d] * w[m]
        outs.append(r)
    return outs


def gate_kernel(groups, squares, pos_ref, s_ref, *refs):
    ins = refs[:groups]
    outs = refs[groups : 2 * groups]
    rest = refs[2 * groups :]
    if squares:
        sum_ref, acc = rest[0], rest[1]
        rest = rest[2:]
        acc[...] = jnp.zeros_like(acc)
    u_scr, o_scr, lim_scr = rest
    me = pos_ref[0]
    loc, ks, wide = ins[0].shape
    count = groups * loc
    main = wide // 2 - HALF
    at = pl.multiple_of(me * ks, ks)
    lim = s_ref[pl.ds(at, ks), :].astype(jnp.float32)
    lim_scr[:, :main] = lim[:, :main]
    lim_scr[:, main:] = jnp.concatenate([lim[:, main:], lim[:, main:]], axis=1)
    for p in range(groups):
        base = share_of(me, p, groups) * loc
        for f in range(loc):
            u_scr[base + f] = ins[p][f]

    def tile(i, carry):
        rows = pl.ds(pl.multiple_of(i * 8, 8), 8)
        for t in range(main // LANES + 1):
            real, imag = gate_weights(lim_scr[rows, t * LANES : (t + 1) * LANES], count)
            if t * LANES < main:
                re_at = slice(t * LANES, (t + 1) * LANES)
                im_at = slice(main + t * LANES, main + (t + 1) * LANES)
                ur = [u_scr[j, rows, re_at] for j in range(count)]
                ui = [u_scr[j, rows, im_at] for j in range(count)]
                out_r, out_i = gate_pair(real, imag, ur, ui)
                for j in range(count):
                    o_scr[j, rows, re_at] = out_r[j]
                    o_scr[j, rows, im_at] = out_i[j]
                    if squares:
                        acc[...] += out_r[j] * out_r[j] + out_i[j] * out_i[j]
            else:
                ends = slice(2 * main, 2 * main + LANES)
                lane = lax.broadcasted_iota(jnp.int32, (8, LANES), 1)
                sign = jnp.where(lane < HALF, -1.0, 1.0)
                signed = [None] + [v * sign for v in imag[1:]]
                out = gate_tail(real, signed, [u_scr[j, rows, ends] for j in range(count)])
                for j in range(count):
                    o_scr[j, rows, ends] = out[j]
                    if squares:
                        acc[...] += out[j] * out[j]
        return carry

    lax.fori_loop(0, ks // 8, tile, 0)
    for p in range(groups):
        base = share_of(me, p, groups) * loc
        for f in range(loc):
            outs[p][f] = o_scr[base + f]
    if squares:
        sum_ref[...] = lane_fold(jnp.sum(acc[...], axis=0, keepdims=True))


def gate(pos, limits, shares, groups, squares):
    loc, ks, wide = shares[0].shape
    out_shape = [jax.ShapeDtypeStruct((loc, ks, wide), jnp.float32)] * groups
    scratch = []
    if squares:
        out_shape = out_shape + [jax.ShapeDtypeStruct((1, LANES), jnp.float32)]
        scratch = [pltpu.VMEM((8, LANES), jnp.float32)]
    scratch = scratch + [
        pltpu.VMEM((groups * loc, ks, wide), jnp.float32),
        pltpu.VMEM((groups * loc, ks, wide), jnp.float32),
        pltpu.VMEM((ks, wide // 2 + HALF), jnp.float32),
    ]
    size = groups * loc * ks * wide
    return pl.pallas_call(
        lambda *refs: gate_kernel(groups, squares, *refs),
        out_shape=out_shape,
        in_specs=[SMEM, VMEM] + [VMEM] * groups,
        out_specs=[VMEM] * len(out_shape),
        scratch_shapes=scratch,
        cost_estimate=cost(40 * size, 8 * size),
        name="gate_sum" if squares else "gate",
    )(pos, limits, *shares)


def ratio(table):
    curvature = jnp.sum(table[:, 0, 0:1], axis=0, keepdims=True)
    gamma = jnp.sum(table[:, 1, 0:1], axis=0, keepdims=True)
    return gamma, curvature


def alpha_of(t_ref):
    gamma = jnp.sum(t_ref[:, 1, :])
    curvature = jnp.sum(t_ref[:, 0, :])
    return gamma / (curvature + tiny), gamma


def blend_kernel(groups, t_ref, *refs):
    alpha, _ = alpha_of(t_ref)
    for p in range(groups):
        refs[2 * groups + p][...] = (refs[p][...] - alpha * refs[groups + p][...]).astype(jnp.bfloat16)


def blend(sums, first, second, groups):
    size = groups * first[0].size
    return pl.pallas_call(
        lambda *refs: blend_kernel(groups, *refs),
        out_shape=[jax.ShapeDtypeStruct(v.shape, jnp.bfloat16) for v in first],
        in_specs=[VMEM] * (1 + 2 * groups),
        out_specs=[VMEM] * groups,
        cost_estimate=cost(2 * size, 10 * size),
        name="blend",
    )(sums, *first, *second)


def join_kernel(groups, pos_ref, *refs):
    me = pos_ref[0]
    ks = refs[0].shape[1]
    for p in range(groups):
        at = pl.multiple_of(share_of(me, p, groups) * ks, ks)
        for f in range(refs[p].shape[0]):
            refs[groups][f, pl.ds(at, ks), :] = refs[p][f]


def join(pos, shares, groups):
    loc, ks, wide = shares[0].shape
    return pl.pallas_call(
        lambda *refs: join_kernel(groups, *refs),
        out_shape=jax.ShapeDtypeStruct((loc, groups * ks, wide), shares[0].dtype),
        in_specs=[SMEM] + [VMEM] * groups,
        out_specs=VMEM,
        cost_estimate=cost(0, 4 * groups * shares[0].size),
        name="join",
    )(pos, *shares)


def store_planes(ref, f, rows, real, imag):
    ref[f, 0, rows, :] = real
    ref[f, 1, rows, :] = imag


def planes_of(row):
    out = []
    for c in range(2):
        out.append(jnp.concatenate(unpack(row, c), axis=1))
    return out


def update_kernel(groups, pos_ref, t_ref, res_ref, foc_ref, dir_ref, *refs):
    image = refs[:groups]
    nres_ref, nfoc_ref = refs[groups:]
    alpha, _ = alpha_of(t_ref)
    me = pos_ref[0]
    loc, ks, _ = image[0].shape
    nfoc_ref[...] = foc_ref[...] + alpha * dir_ref[...]
    for p in range(groups):
        rows = pl.ds(pl.multiple_of(share_of(me, p, groups) * ks, ks), ks)
        for f in range(loc):
            real, imag = planes_of(image[p][f])
            nres_ref[f, 0, rows, :] = res_ref[f, 0, rows, :] - alpha * real
            nres_ref[f, 1, rows, :] = res_ref[f, 1, rows, :] - alpha * imag


def update(pos, sums, residual, focusing, direction, image, groups):
    size = residual.size
    return pl.pallas_call(
        lambda *refs: update_kernel(groups, *refs),
        out_shape=[jax.ShapeDtypeStruct(residual.shape, jnp.float32)] * 2,
        in_specs=[SMEM] + [VMEM] * (4 + groups),
        out_specs=[VMEM] * 2,
        cost_estimate=cost(4 * size, 24 * size),
        name="update",
    )(pos, sums, residual, focusing, direction, *image)


def green_kernel(groups, pos_ref, t_ref, nfoc_ref, *refs):
    di, image, fi, kept = [refs[i * groups : (i + 1) * groups] for i in range(4)]
    green_ref, corr_ref = refs[4 * groups :]
    alpha, _ = alpha_of(t_ref)
    me = pos_ref[0]
    loc, ks, _ = di[0].shape
    for p in range(groups):
        rows = pl.ds(pl.multiple_of(share_of(me, p, groups) * ks, ks), ks)
        for f in range(loc):
            row = (fi[p][f] - kept[p][f]) + alpha * (di[p][f] - image[p][f])
            real, imag = planes_of(row)
            green_ref[f, 0, rows, :] = real
            green_ref[f, 1, rows, :] = imag
            fr = nfoc_ref[f, 0, rows, :]
            fm = nfoc_ref[f, 1, rows, :]
            corr_ref[f, 0, rows, :] = jnp.sum(real * fr + imag * fm, axis=1, keepdims=True)
            corr_ref[f, 1, rows, :] = jnp.sum(imag * fr - real * fm, axis=1, keepdims=True)


def green(pos, sums, new_focusing, di, image, fi, kept, groups):
    loc, _, k, n = new_focusing.shape
    size = new_focusing.size
    return pl.pallas_call(
        lambda *refs: green_kernel(groups, *refs),
        out_shape=[
            jax.ShapeDtypeStruct(new_focusing.shape, jnp.float32),
            jax.ShapeDtypeStruct((loc, 2, k, 1), jnp.float32),
        ],
        in_specs=[SMEM] + [VMEM] * (2 + 4 * groups),
        out_specs=[VMEM] * 2,
        cost_estimate=cost(10 * size, 24 * size),
        name="green",
    )(pos, sums, new_focusing, *di, *image, *fi, *kept)


def turn_kernel(t_ref, g_ref, new_ref, dir_ref, out_ref):
    _, gamma = alpha_of(t_ref)
    scale = jnp.sum(g_ref[...]) / (gamma + tiny)
    out_ref[...] = new_ref[...] + scale * dir_ref[...]


def turn(sums, new_sums, new_gradient, direction):
    size = direction.size
    return pl.pallas_call(
        turn_kernel,
        out_shape=jax.ShapeDtypeStruct(direction.shape, jnp.float32),
        in_specs=[VMEM] * 4,
        out_specs=VMEM,
        cost_estimate=cost(2 * size, 12 * size),
        name="turn",
    )(sums, new_sums, new_gradient, direction)


def exchange(shares, groups):
    out = [shares[0]]
    for p in range(1, groups):
        pairs = [(m, share_of(m, p, groups) if groups & (groups - 1) == 0 else (p - m) % groups) for m in range(groups)]
        out.append(lax.ppermute(shares[p], "freq", pairs))
    return out


def side(deep, pick):
    pairs = []
    for z in range(deep):
        for y in range(2):
            to = pick(z, y)
            if to is not None:
                pairs.append((z * 2 + y, to[0] * 2 + to[1]))
    return pairs


def spread(own, mid):
    swap = side(4, lambda z, y: (z, 1 - y))
    near = side(4, lambda z, y: (z ^ 1, y))
    centre = side(4, lambda z, y: (3 - z, y) if z in (1, 2) else None)
    outward = side(4, lambda z, y: (0 if z == 1 else 3, y) if z in (1, 2) else None)
    move = lambda v, pairs: lax.ppermute(v, "rcv", pairs)
    n1 = move(own, near)
    c1 = move(own, centre)
    y0 = move(own, swap)
    o1 = move(c1, outward)
    c2 = move(n1, centre)
    y1 = move(n1, swap)
    m1 = jnp.where(mid, c1, o1)
    o2 = move(c2, outward)
    y2 = move(m1, swap)
    m2 = jnp.where(mid, c2, o2)
    y3 = move(m2, swap)
    return [own, y0, n1, y1, m1, y2, m2, y3]


def total_over_all(row, devices):
    sent = jnp.broadcast_to(row[None], (devices,) + row.shape)
    return lax.all_to_all(sent, ("freq", "rcv"), split_axis=0, concat_axis=0, tiled=True)


def per_device(reflection, starts, focusing, residual, direction, gradient):
    groups = lax.axis_size("freq")
    ranks = lax.axis_size("rcv")
    positions = reflection.shape[3]
    lay = lambda v: jnp.transpose(v, (0, 2, 3, 1))
    focusing, residual, direction, gradient = map(lay, (focusing, residual, direction, gradient))
    limits = jnp.transpose(starts, (1, 0))
    me = lax.axis_index("freq")
    rank = lax.axis_index("rcv")
    z, y = rank // 2, rank % 2
    mid = (z == 1) | (z == 2)
    far1 = jnp.where(z < 2, 2, 1)
    far2 = jnp.where(z < 2, 3, 0)
    pos = jnp.stack([me, y, z, z ^ 1, far1, far2]).astype(jnp.int32)

    dir_blocks = spread(prep_low(direction), mid)
    *res_shares, gamma_row = prep_shares(pos, residual, gradient, groups)
    res_there = exchange(res_shares, groups)
    kept_res = gate(pos, limits, res_there, groups, False)

    di = product(pos, reflection, dir_blocks, groups, False)
    *image_there, curv_row = gate(pos, limits, exchange(di, groups), groups, True)
    sums = total_over_all(jnp.concatenate([curv_row, gamma_row], axis=0), groups * ranks)
    twice = gate(pos, limits, image_there, groups, False)
    gated_there = blend(sums, kept_res, twice, groups)
    gated = join(pos, exchange(gated_there, groups), groups)
    gated_blocks = spread(gated, mid)

    foc_blocks = spread(prep_low(focusing), mid)
    fi = product(pos, reflection, foc_blocks, groups, False)
    kept = exchange(gate(pos, limits, exchange(fi, groups), groups, False), groups)
    image = exchange(image_there, groups)
    new_residual, new_focusing = update(pos, sums, residual, focusing, direction, image, groups)
    green_field, corr = green(pos, sums, new_focusing, di, image, fi, kept, groups)
    corr = corr[..., 0]
    corr = lax.all_to_all(
        jnp.broadcast_to(corr[None], (ranks,) + corr.shape), "rcv", split_axis=0, concat_axis=0, tiled=True
    )
    focal_correlation = jnp.sum(corr, axis=0) / math.sqrt(positions)

    new_gradient, new_row = product(pos, reflection, gated_blocks, groups, True)
    new_sums = total_over_all(new_row, groups * ranks)
    new_direction = turn(sums, new_sums, new_gradient, direction)
    back = lambda v: jnp.transpose(v, (0, 3, 1, 2))
    return (back(new_focusing), back(new_residual), back(new_direction), back(green_field), focal_correlation)


def chosen(mesh):
    def run(reflection, starts, *fields):
        rows, points = starts.shape
        suits = (
            mesh.shape["rcv"] == 8
            and rows % LANES == HALF
            and rows > LANES
            and points % (16 * mesh.shape["freq"]) == 0
        )
        plan = per_device if suits else per_device_general
        return plan(reflection, starts, *fields)

    return run


def solution(mesh):
    return jax.shard_map(
        chosen(mesh),
        mesh=mesh,
        in_specs=(
            P("freq", None, "rcv", None),
            P("rcv", None),
            P("freq", "rcv", None, None),
            P("freq", "rcv", None, None),
            P("freq", "rcv", None, None),
            P("freq", "rcv", None, None),
        ),
        out_specs=(
            P("freq", "rcv", None, None),
            P("freq", "rcv", None, None),
            P("freq", "rcv", None, None),
            P("freq", "rcv", None, None),
            P("freq", None, None),
        ),
        check_vma=False,
    )
```

```python
import math

import jax
import jax.numpy as jnp
from jax import lax
from jax.experimental import pallas as pl
from jax.experimental.pallas import tpu as pltpu
from jax.sharding import PartitionSpec as P


TS = 64
band_start = 5
tiny = 1e-06
highest = lax.Precision.HIGHEST
LANES = 128
HALF = 64
SINE = [(-1.0) ** i / math.factorial(2 * i + 1) for i in range(7)]
COSINE = [(-1.0) ** i / math.factorial(2 * i) for i in range(8)]


VMEM = pl.BlockSpec(memory_space=pltpu.VMEM)
SMEM = pl.BlockSpec(memory_space=pltpu.SMEM)
ANY = pl.BlockSpec(memory_space=pl.ANY)


def tables(count):
    times = jnp.arange(TS, dtype=jnp.float32)[:, None]
    bins = (jnp.arange(count, dtype=jnp.int32) + band_start).astype(jnp.float32)[None, :]
    phase = 2.0 * jnp.pi * times * bins / TS
    return (jnp.cos(phase), jnp.sin(phase))


def contract_time(table, values):
    return jnp.einsum("tf,frk->trk", table, values, precision=highest)


def contract_back(table, values):
    return jnp.einsum("tf,trk->frk", table, values, precision=highest)


def time_gate(field, cos_table, sin_table, limits, complement):
    real_part = field[:, :, 0]
    imag_part = field[:, :, 1]
    time_real = contract_time(cos_table, real_part) - contract_time(sin_table, imag_part)
    time_imag = contract_time(sin_table, real_part) + contract_time(cos_table, imag_part)
    clock = jnp.arange(TS, dtype=jnp.int32)[:, None, None]
    window = (clock < limits[None]).astype(jnp.float32)
    if complement:
        window = 1.0 - window
    kept_real = window * time_real
    kept_imag = window * time_imag
    out_real = (contract_back(cos_table, kept_real) + contract_back(sin_table, kept_imag)) / TS
    out_imag = (contract_back(cos_table, kept_imag) - contract_back(sin_table, kept_real)) / TS
    return jnp.stack([out_real, out_imag], axis=2)


def combine(total, conjugate):
    if conjugate:
        out_real = total[:, 0, :, 0] + total[:, 1, :, 1]
        out_imag = total[:, 0, :, 1] - total[:, 1, :, 0]
    else:
        out_real = total[:, 0, :, 0] - total[:, 1, :, 1]
        out_imag = total[:, 0, :, 1] + total[:, 1, :, 0]
    return jnp.stack([out_real, out_imag], axis=2)


def per_device_general(reflection, starts, focusing, residual, direction, gradient):
    local_rows = reflection.shape[2]
    positions = reflection.shape[3]
    groups = lax.axis_size("freq")
    position = lax.axis_index("freq")
    cos_table, sin_table = tables(reflection.shape[0] * groups)

    def gate(field, complement):
        spread = lax.all_to_all(field, "freq", split_axis=1, concat_axis=0, tiled=True)
        share = local_rows // groups
        limits = lax.dynamic_slice_in_dim(starts, position * share, share, 0)
        gated_part = time_gate(spread, cos_table, sin_table, limits, complement)
        return lax.all_to_all(gated_part, "freq", split_axis=0, concat_axis=1, tiled=True)

    def accumulate(piece):
        return jnp.einsum("fpnm,fmqk->fpnqk", reflection, piece, preferred_element_type=jnp.float32)

    direction_low = direction.astype(jnp.bfloat16)
    focusing_low = focusing.astype(jnp.bfloat16)
    aimed_total = accumulate(lax.all_gather(direction_low, "rcv", axis=1, tiled=True))
    direction_image = combine(aimed_total, False)
    gamma = lax.psum(jnp.sum(gradient * gradient), ("freq", "rcv"))
    image = gate(direction_image, False)
    curvature = lax.psum(jnp.sum(image * image), ("freq", "rcv"))
    alpha = gamma / (curvature + tiny)
    new_focusing = focusing + alpha * direction
    new_residual = residual - alpha * image
    gated = gate(new_residual, False).astype(jnp.bfloat16)
    total = accumulate(lax.all_gather(gated, "rcv", axis=1, tiled=True))
    new_gradient = combine(total, True)
    new_gamma = lax.psum(jnp.sum(new_gradient * new_gradient), ("freq", "rcv"))
    new_direction = new_gradient + new_gamma / (gamma + tiny) * direction
    focus_total = accumulate(lax.all_gather(focusing_low, "rcv", axis=1, tiled=True))
    focusing_image = combine(focus_total, False)
    green_field = gate(focusing_image + alpha * direction_image, True)
    corr_real = jnp.sum(
        green_field[:, :, 0] * new_focusing[:, :, 0] + green_field[:, :, 1] * new_focusing[:, :, 1],
        axis=1,
    )
    corr_imag = jnp.sum(
        green_field[:, :, 1] * new_focusing[:, :, 0] - green_field[:, :, 0] * new_focusing[:, :, 1],
        axis=1,
    )
    partial_corr = jnp.stack([corr_real, corr_imag], axis=1)
    focal_correlation = lax.psum(partial_corr, "rcv") / math.sqrt(positions)
    return (new_focusing, new_residual, new_direction, green_field, focal_correlation)


def split_row(x, odd):
    main = x.shape[-1] - HALF
    return (x[:, HALF:], x[:, :HALF]) if odd else (x[:, :main], x[:, main:])


def pack(real, imag, odd):
    (r_main, r_tail), (i_main, i_tail) = split_row(real, odd), split_row(imag, odd)
    return jnp.concatenate([r_main, i_main, jnp.concatenate([r_tail, i_tail], axis=1)], axis=1)


def unpack(row, plane, odd):
    main = row.shape[-1] // 2 - HALF
    tail = 2 * main + plane * HALF
    parts = [row[:, plane * main : (plane + 1) * main], row[:, tail : tail + HALF]]
    return jnp.concatenate(parts[::-1] if odd else parts, axis=1)


def by_parity(pos_ref, body):
    for odd in range(2):
        pl.when(pos_ref[1] == odd)(lambda odd=odd: body(odd))


def cost(flops, size):
    return pl.CostEstimate(flops=int(flops), bytes_accessed=int(size), transcendentals=0)


def prep_low_kernel(pos_ref, x_ref, o_ref):
    def body(odd):
        for f in range(x_ref.shape[0]):
            o_ref[f] = pack(x_ref[f, 0], x_ref[f, 1], odd).astype(jnp.bfloat16)

    by_parity(pos_ref, body)


def prep_low(pos, x):
    loc, _, k, n = x.shape
    return pl.pallas_call(
        prep_low_kernel,
        out_shape=jax.ShapeDtypeStruct((loc, k, 2 * n), jnp.bfloat16),
        in_specs=[SMEM, VMEM],
        out_specs=VMEM,
        cost_estimate=cost(x.size, 6 * x.size),
        name="prep_low",
    )(pos, x)


def share_of(me, p, groups):
    if groups & (groups - 1) == 0:
        return me ^ p
    return lax.rem(p - me + groups, groups)


def prep_shares_kernel(groups, pos_ref, x_ref, g_ref, *o_refs):
    me = pos_ref[0]
    ks = x_ref.shape[2] // groups

    def body(odd):
        for p in range(groups):
            at = pl.multiple_of(share_of(me, p, groups) * ks, ks)
            for f in range(x_ref.shape[0]):
                real, imag = x_ref[f, 0, pl.ds(at, ks), :], x_ref[f, 1, pl.ds(at, ks), :]
                o_refs[p][f] = pack(real, imag, odd)

    by_parity(pos_ref, body)
    total = jnp.zeros((8, g_ref.shape[3]), jnp.float32)
    for f in range(g_ref.shape[0]):
        for c in range(2):
            for r in range(0, g_ref.shape[2], 8):
                v = g_ref[f, c, r : r + 8, :]
                total = total + v * v
    o_refs[groups][...] = lane_fold(jnp.sum(total, axis=0, keepdims=True))


def lane_fold(row, width=LANES):
    out = jnp.sum(row, axis=1, keepdims=True)
    lane = lax.broadcasted_iota(jnp.int32, (1, width), 1)
    return jnp.where(lane == 0, out, 0.0)


def prep_shares(pos, x, g, groups):
    loc, _, k, n = x.shape
    outs = [jax.ShapeDtypeStruct((loc, k // groups, 2 * n), jnp.float32)] * groups
    return pl.pallas_call(
        lambda *refs: prep_shares_kernel(groups, *refs),
        out_shape=outs + [jax.ShapeDtypeStruct((1, LANES), jnp.float32)],
        in_specs=[SMEM, VMEM, VMEM],
        out_specs=[VMEM] * (groups + 1),
        cost_estimate=cost(3 * x.size, 12 * x.size),
        name="prep_shares",
    )(pos, x, g)


def product_kernel(groups, count, conjugate, pos_ref, r_ref, *refs):
    blocks, refs = refs[: 2 * count], refs[2 * count :]
    v_scr, acc = refs[-2:]
    f = pl.program_id(0)
    _, kc, wide = blocks[0].shape
    rows = r_ref.shape[2]
    main = wide // 2 - HALF

    def load(odd):
        for b in range(count):
            even = blocks[2 * b + odd]
            other = blocks[2 * b + 1 - odd]
            at = pos_ref[2 + b] * wide
            for c in range(2):
                here = slice(c * kc, (c + 1) * kc)
                half = slice(2 * main + c * HALF, 2 * main + (c + 1) * HALF)
                lanes = lambda shift, size: pl.ds(pl.multiple_of(at + shift, LANES), size)
                v_scr[here, lanes(0, main)] = even[0, :, c * main : (c + 1) * main]
                middle = [even[0, :, half], other[0, :, half]]
                v_scr[here, lanes(main, LANES)] = jnp.concatenate(middle, axis=1)
                v_scr[here, lanes(main + LANES, main)] = other[0, :, c * main : (c + 1) * main]

    by_parity(pos_ref, load)
    both = r_ref[0].reshape(2 * rows, r_ref.shape[3])
    dims = (((1,), (1,)), ((), ()))
    acc[...] = lax.dot_general(v_scr[...], both, dims, preferred_element_type=jnp.float32)
    if not conjugate:
        me = pos_ref[0]
        ks = kc // groups

        def finish(odd):
            for p in range(groups):
                at = pl.multiple_of(share_of(me, p, groups) * ks, ks)
                real = acc[pl.ds(at, ks), :rows] - acc[pl.ds(at + kc, ks), rows:]
                imag = acc[pl.ds(at + kc, ks), :rows] + acc[pl.ds(at, ks), rows:]
                refs[p][0] = pack(real, imag, odd)

        by_parity(pos_ref, finish)
    else:
        new_ref, row_ref, sum_scr = refs[:3]
        real = acc[:kc, :rows] + acc[kc:, rows:]
        imag = acc[kc:, :rows] - acc[:kc, rows:]
        new_ref[0, 0] = real
        new_ref[0, 1] = imag
        part = jnp.sum(real * real + imag * imag, axis=0, keepdims=True)

        @pl.when(f == 0)
        def _():
            sum_scr[...] = part

        @pl.when(f > 0)
        def _():
            sum_scr[...] += part

        @pl.when(f == pl.num_programs(0) - 1)
        def _():
            row_ref[...] = lane_fold(sum_scr[...])


def product(pos, reflection, blocks, groups, back=False):
    loc, _, rows, cols = reflection.shape
    kc, wide = blocks[0].shape[1:]
    count = len(blocks) // 2
    whole = lambda *tail: pl.BlockSpec((1,) + tail, lambda f, pos: (f,) + (0,) * len(tail))
    fixed = lambda *shape: pl.BlockSpec(shape, lambda f, pos: (0,) * len(shape))
    in_specs = [whole(2, rows, cols)] + [whole(kc, wide)] * (2 * count)
    operands = [pos, reflection] + list(blocks)
    scratch = []
    if not back:
        ks = kc // groups
        out_shape = [jax.ShapeDtypeStruct((loc, ks, wide), jnp.float32)] * groups
        out_specs = [whole(ks, wide)] * groups
    else:
        out_shape = [
            jax.ShapeDtypeStruct((loc, 2, kc, rows), jnp.float32),
            jax.ShapeDtypeStruct((1, LANES), jnp.float32),
        ]
        out_specs = [whole(2, kc, rows), fixed(1, LANES)]
        scratch = [pltpu.VMEM((1, rows), jnp.float32)]
    return pl.pallas_call(
        lambda *refs: product_kernel(groups, count, back, *refs),
        grid_spec=pltpu.PrefetchScalarGridSpec(
            num_scalar_prefetch=1,
            grid=(loc,),
            in_specs=in_specs,
            out_specs=out_specs,
            scratch_shapes=scratch
            + [
                pltpu.VMEM((2 * kc, cols), jnp.bfloat16),
                pltpu.VMEM((2 * kc, 2 * rows), jnp.float32),
            ],
        ),
        out_shape=out_shape,
        cost_estimate=cost(8 * loc * rows * kc * cols, 2 * reflection.size + 4 * loc * kc * cols),
        compiler_params=pltpu.CompilerParams(dimension_semantics=("arbitrary",)),
        name="product_back" if back else "product",
    )(*operands)


def turn_of(limit):
    x = (limit - TS / 2) * (math.pi / TS)
    y = x * x
    sine = jnp.full_like(y, SINE[-1])
    for v in SINE[-2::-1]:
        sine = sine * y + v
    sine = sine * x
    cosine = jnp.full_like(y, COSINE[-1])
    for v in COSINE[-2::-1]:
        cosine = cosine * y + v
    return 2.0 * sine * sine - 1.0, -2.0 * sine * cosine


def gate_weights(limit, count):
    c1, s1 = turn_of(limit)
    real = [limit * (1.0 / TS)]
    imag = [None]
    c, s = c1, s1
    for d in range(1, count):
        half_cot = 0.5 / math.tan(math.pi * d / TS)
        rest = 1.0 - c
        real.append((0.5 * rest + half_cot * s) * (1.0 / TS))
        imag.append((half_cot * rest - 0.5 * s) * (1.0 / TS))
        c, s = c * c1 - s * s1, s * c1 + c * s1
    return real, imag


def gate_pair(real, imag, ur, ui):
    count = len(ur)
    out_r, out_i = [], []
    for j in range(count):
        r = real[0] * ur[j]
        i = real[0] * ui[j]
        for m in range(count):
            d = abs(m - j)
            if m > j:
                r = r + real[d] * ur[m] - imag[d] * ui[m]
                i = i + real[d] * ui[m] + imag[d] * ur[m]
            elif m < j:
                r = r + real[d] * ur[m] + imag[d] * ui[m]
                i = i + real[d] * ui[m] - imag[d] * ur[m]
        out_r.append(r)
        out_i.append(i)
    return out_r, out_i


def gate_tail(real, signed, u):
    count = len(u)
    w = [pltpu.roll(v, HALF, 1) for v in u]
    outs = []
    for j in range(count):
        r = real[0] * u[j]
        for m in range(count):
            d = abs(m - j)
            if m > j:
                r = r + real[d] * u[m] + signed[d] * w[m]
            elif m < j:
                r = r + real[d] * u[m] - signed[d] * w[m]
        outs.append(r)
    return outs


def gate_kernel(groups, squares, mixed, pos_ref, s_ref, *refs):
    if squares:
        row_ref, refs = refs[0], refs[1:]
    if mixed:
        t_ref, bases, refs = refs[0], refs[1 : 1 + groups], refs[1 + groups :]
    ins = refs[:groups]
    outs = refs[groups : 2 * groups]
    rest = refs[2 * groups :]
    if squares:
        sum_ref, acc = rest[0], rest[1]
        rest = rest[2:]
        acc[...] = jnp.zeros_like(acc)
    u_scr, o_scr, lim_scr = rest
    me = pos_ref[0]
    loc, ks, wide = ins[0].shape
    count = groups * loc
    main = wide // 2 - HALF
    at = pl.multiple_of(me * ks, ks)
    lim = jnp.clip(s_ref[pl.ds(at, ks), :], 0, TS).astype(jnp.float32)

    def place(odd):
        whole, ends = split_row(lim, odd)
        lim_scr[:, :main] = whole
        lim_scr[:, main:] = jnp.concatenate([ends, ends], axis=1)

    by_parity(pos_ref, place)
    for p in range(groups):
        base = share_of(me, p, groups) * loc
        for f in range(loc):
            u_scr[base + f] = ins[p][f]

    def tile(i, carry):
        rows = pl.ds(pl.multiple_of(i * 8, 8), 8)
        for t in range(main // LANES + 1):
            real, imag = gate_weights(lim_scr[rows, t * LANES : (t + 1) * LANES], count)
            if t * LANES < main:
                re_at = slice(t * LANES, (t + 1) * LANES)
                im_at = slice(main + t * LANES, main + (t + 1) * LANES)
                ur = [u_scr[j, rows, re_at] for j in range(count)]
                ui = [u_scr[j, rows, im_at] for j in range(count)]
                out_r, out_i = gate_pair(real, imag, ur, ui)
                for j in range(count):
                    o_scr[j, rows, re_at] = out_r[j]
                    o_scr[j, rows, im_at] = out_i[j]
                    if squares:
                        acc[...] += out_r[j] * out_r[j] + out_i[j] * out_i[j]
            else:
                ends = slice(2 * main, 2 * main + LANES)
                lane = lax.broadcasted_iota(jnp.int32, (8, LANES), 1)
                sign = jnp.where(lane < HALF, -1.0, 1.0)
                signed = [None] + [v * sign for v in imag[1:]]
                out = gate_tail(real, signed, [u_scr[j, rows, ends] for j in range(count)])
                for j in range(count):
                    o_scr[j, rows, ends] = out[j]
                    if squares:
                        acc[...] += out[j] * out[j]
        return carry

    lax.fori_loop(0, ks // 8, tile, 0)
    for p in range(groups):
        base = share_of(me, p, groups) * loc
        for f in range(loc):
            if mixed:
                mix = bases[p][f] - alpha_of(t_ref)[0] * o_scr[base + f]
                outs[p][f] = mix.astype(jnp.bfloat16)
            else:
                outs[p][f] = o_scr[base + f]
    if squares:
        mine = lane_fold(jnp.sum(acc[...], axis=0, keepdims=True))
        both = jnp.concatenate([mine, row_ref[...]], axis=0)
        sum_ref[...] = jnp.broadcast_to(both[None], sum_ref.shape)


def gate(pos, limits, shares, groups, row=None, devices=0, sums=None, bases=()):
    squares = row is not None
    loc, ks, wide = shares[0].shape
    kind = jnp.bfloat16 if bases else jnp.float32
    out_shape = [jax.ShapeDtypeStruct((loc, ks, wide), kind)] * groups
    scratch = []
    more = []
    if squares:
        out_shape = out_shape + [jax.ShapeDtypeStruct((devices, 2, LANES), jnp.float32)]
        scratch = [pltpu.VMEM((8, LANES), jnp.float32)]
        more = [row]
    if bases:
        more = [sums, *bases]
    scratch = scratch + [
        pltpu.VMEM((groups * loc, ks, wide), jnp.float32),
        pltpu.VMEM((groups * loc, ks, wide), jnp.float32),
        pltpu.VMEM((ks, wide // 2 + HALF), jnp.float32),
    ]
    size = groups * loc * ks * wide
    return pl.pallas_call(
        lambda *refs: gate_kernel(groups, squares, bool(bases), *refs),
        out_shape=out_shape,
        in_specs=[SMEM, VMEM] + [VMEM] * (groups + len(more)),
        out_specs=[VMEM] * len(out_shape),
        scratch_shapes=scratch,
        cost_estimate=cost(40 * size, 8 * size),
        name="gate_sum" if squares else "gate_mix" if bases else "gate",
    )(pos, limits, *more, *shares)


def alpha_of(t_ref):
    gamma = jnp.sum(t_ref[:, 1, :])
    curvature = jnp.sum(t_ref[:, 0, :])
    return gamma / (curvature + tiny), gamma


def join_kernel(groups, pos_ref, *refs):
    me = pos_ref[0]
    ks = refs[0].shape[1]
    for p in range(groups):
        at = pl.multiple_of(share_of(me, p, groups) * ks, ks)
        for f in range(refs[p].shape[0]):
            refs[groups][f, pl.ds(at, ks), :] = refs[p][f]


def join(pos, shares, groups):
    loc, ks, wide = shares[0].shape
    return pl.pallas_call(
        lambda *refs: join_kernel(groups, *refs),
        out_shape=jax.ShapeDtypeStruct((loc, groups * ks, wide), shares[0].dtype),
        in_specs=[SMEM] + [VMEM] * groups,
        out_specs=VMEM,
        cost_estimate=cost(0, 4 * groups * shares[0].size),
        name="join",
    )(pos, *shares)


def finish_kernel(groups, pos_ref, t_ref, res_ref, foc_ref, dir_ref, *refs):
    row_ref, refs = refs[0], refs[1:]
    image, kept, di, fi = [refs[i * groups : (i + 1) * groups] for i in range(4)]
    nres_ref, nfoc_ref, green_ref, sent_ref, corr_scr = refs[4 * groups :]
    alpha, _ = alpha_of(t_ref)
    me = pos_ref[0]
    loc, ks, _ = di[0].shape
    nfoc_ref[...] = foc_ref[...] + alpha * dir_ref[...]

    def body(odd):
        for p in range(groups):
            rows = pl.ds(pl.multiple_of(share_of(me, p, groups) * ks, ks), ks)
            for f in range(loc):
                seen = image[p][f]
                row = (fi[p][f] - kept[p][f]) + alpha * (di[p][f] - seen)
                for c in range(2):
                    green_ref[f, c, rows, :] = unpack(row, c, odd)
                    nres_ref[f, c, rows, :] = res_ref[f, c, rows, :] - alpha * unpack(seen, c, odd)

    by_parity(pos_ref, body)
    ones = jnp.ones((8, dir_ref.shape[3]), jnp.float32)
    dims = (((1,), (1,)), ((), ()))
    for f in range(loc):
        gr, gi, fr, fm = green_ref[f, 0], green_ref[f, 1], nfoc_ref[f, 0], nfoc_ref[f, 1]
        for c, value in enumerate((gr * fr + gi * fm, gi * fr - gr * fm)):
            line = lax.dot_general(ones, value, dims, precision=highest, preferred_element_type=jnp.float32)
            corr_scr[2 * f + c : 2 * f + c + 1, :] = line[:1]
    total = jnp.broadcast_to(row_ref[:, :HALF], (2 * loc, HALF))
    ends = jnp.concatenate([corr_scr[:, LANES:], total], axis=1)
    table = jnp.concatenate([corr_scr[:, :LANES], ends], axis=0)
    sent_ref[...] = jnp.broadcast_to(table[None], sent_ref.shape)


def finish(pos, sums, residual, focusing, direction, row, image, kept, di, fi, groups):
    loc, _, k, _ = residual.shape
    size = residual.size
    return pl.pallas_call(
        lambda *refs: finish_kernel(groups, *refs),
        out_shape=[jax.ShapeDtypeStruct(residual.shape, jnp.float32)] * 3
        + [jax.ShapeDtypeStruct((sums.shape[0], 4 * loc, LANES), jnp.float32)],
        in_specs=[SMEM] + [VMEM] * (5 + 4 * groups),
        out_specs=[VMEM] * 4,
        scratch_shapes=[pltpu.VMEM((2 * loc, k), jnp.float32)],
        cost_estimate=cost(14 * size, 40 * size),
        name="finish",
    )(pos, sums, residual, focusing, direction, row, *image, *kept, *di, *fi)


def turn(pos, sums, new_sums, new_gradient, direction, ranks):
    loc, _, points, n = direction.shape
    size = direction.size
    lines = 2 * loc
    scale = 1.0 / math.sqrt(n * ranks)

    def body(pos_ref, t_ref, g_ref, new_ref, dir_ref, out_ref, corr_ref):
        _, gamma = alpha_of(t_ref)
        beta = jnp.sum(g_ref[:, lines, HALF:]) / (gamma + tiny)
        out_ref[...] = new_ref[...] + beta * dir_ref[...]
        total = jnp.zeros((2 * lines, LANES), jnp.float32)
        for r in range(ranks):
            total = total + g_ref[pos_ref[0] * ranks + r]
        total = jnp.concatenate([total[:lines], total[lines:, :HALF]], axis=1) * scale
        for f in range(loc):
            corr_ref[f] = total[2 * f : 2 * f + 2]

    return pl.pallas_call(
        body,
        in_specs=[SMEM] + [VMEM] * 4,
        out_specs=[VMEM] * 2,
        out_shape=[
            jax.ShapeDtypeStruct(direction.shape, jnp.float32),
            jax.ShapeDtypeStruct((loc, 2, points), jnp.float32),
        ],
        cost_estimate=cost(2 * size, 12 * size),
        name="turn",
    )(pos, sums, new_sums, new_gradient, direction)


def exchange(shares, groups):
    out = [shares[0]]
    for p in range(1, groups):
        pairs = [(m, share_of(m, p, groups) if groups & (groups - 1) == 0 else (p - m) % groups) for m in range(groups)]
        out.append(lax.ppermute(shares[p], "freq", pairs))
    return out


def side(deep, pick):
    pairs = []
    for z in range(deep):
        for y in range(2):
            to = pick(z, y)
            if to is not None:
                pairs.append((z * 2 + y, to[0] * 2 + to[1]))
    return pairs


def spread(own, mid):
    swap = side(4, lambda z, y: (z, 1 - y))
    near = side(4, lambda z, y: (z ^ 1, y))
    centre = side(4, lambda z, y: (3 - z, y) if z in (1, 2) else None)
    outward = side(4, lambda z, y: (0 if z == 1 else 3, y) if z in (1, 2) else None)

    def move(v, pairs):
        return lax.ppermute(v, "rcv", pairs)

    n1 = move(own, near)
    c1 = move(own, centre)
    y0 = move(own, swap)
    c2 = move(n1, centre)
    y1 = move(n1, swap)
    o1 = move(c1, outward)
    before = yield
    if before is not None:
        c2, o1, before = lax.optimization_barrier((c2, o1, before))
    yield before
    m1 = jnp.where(mid, c1, o1)
    y2 = move(m1, swap)
    o2 = move(c2, outward)
    m2 = jnp.where(mid, c2, o2)
    y3 = move(m2, swap)
    yield [own, y0, n1, y1, m1, y2, m2, y3]


def spread_all(own, mid):
    return list(spread(own, mid))[-1]


def total_over_all(sent):
    return lax.all_to_all(sent, ("freq", "rcv"), split_axis=0, concat_axis=0, tiled=True)


def per_device(reflection, starts, focusing, residual, direction, gradient):
    groups = lax.axis_size("freq")
    ranks = lax.axis_size("rcv")
    lay = lambda v: jnp.transpose(v, (0, 2, 3, 1))
    focusing, residual, direction, gradient = map(lay, (focusing, residual, direction, gradient))
    limits = jnp.transpose(starts, (1, 0))
    me = lax.axis_index("freq")
    rank = lax.axis_index("rcv")
    z, y = rank // 2, rank % 2
    mid = (z == 1) | (z == 2)
    far1 = jnp.where(z < 2, 2, 1)
    far2 = jnp.where(z < 2, 3, 0)
    pos = jnp.stack([me, y, z, z ^ 1, far1, far2]).astype(jnp.int32)

    blocks = spread_all(prep_low(pos, direction), mid)
    *res_shares, gamma_row = prep_shares(pos, residual, gradient, groups)
    res_there = exchange(res_shares, groups)
    kept_res = gate(pos, limits, res_there, groups)
    foc_own = prep_low(pos, focusing)
    aside = spread(foc_own, mid)
    next(aside)
    di = product(pos, reflection, blocks, groups)
    *image_there, sent = gate(pos, limits, exchange(di, groups), groups, gamma_row, groups * ranks)
    sums = total_over_all(sent)
    sums = aside.send(sums)
    foc = next(aside)
    gated_there = gate(pos, limits, image_there, groups, sums=sums, bases=kept_res)
    gated = join(pos, exchange(gated_there, groups), groups)
    blocks = spread_all(gated, mid)

    fi = product(pos, reflection, foc, groups)
    kept = gate(pos, limits, exchange(fi, groups), groups)
    kept = exchange(kept, groups)
    image = exchange(image_there, groups)
    new_gradient, row = product(pos, reflection, blocks, groups, True)
    new_residual, new_focusing, green_field, new_sent = finish(
        pos, sums, residual, focusing, direction, row, image, kept, di, fi, groups
    )
    new_sums = total_over_all(new_sent)
    new_direction, focal_correlation = turn(pos, sums, new_sums, new_gradient, direction, ranks)
    back = lambda v: jnp.transpose(v, (0, 3, 1, 2))
    return (back(new_focusing), back(new_residual), back(new_direction), back(green_field), focal_correlation)


def chosen(mesh):
    def run(reflection, starts, *fields):
        rows, points = starts.shape
        suits = (
            mesh.shape["rcv"] == 8
            and rows % LANES == HALF
            and rows > LANES
            and points % (16 * mesh.shape["freq"]) == 0
            and points == LANES + HALF
        )
        plan = per_device if suits else per_device_general
        return plan(reflection, starts, *fields)

    return run


def solution(mesh):
    return jax.shard_map(
        chosen(mesh),
        mesh=mesh,
        in_specs=(
            P("freq", None, "rcv", None),
            P("rcv", None),
            P("freq", "rcv", None, None),
            P("freq", "rcv", None, None),
            P("freq", "rcv", None, None),
            P("freq", "rcv", None, None),
        ),
        out_specs=(
            P("freq", "rcv", None, None),
            P("freq", "rcv", None, None),
            P("freq", "rcv", None, None),
            P("freq", "rcv", None, None),
            P("freq", None, None),
        ),
        check_vma=False,
    )
```

```python
import math

import jax
import jax.numpy as jnp
from jax import lax
from jax.experimental import pallas as pl
from jax.experimental.pallas import tpu as pltpu
from jax.sharding import PartitionSpec as P


TS = 64
band_start = 5
tiny = 1e-06
highest = lax.Precision.HIGHEST
LANES = 128
HALF = 64
SINE = [(-1.0) ** i / math.factorial(2 * i + 1) for i in range(7)]
COSINE = [(-1.0) ** i / math.factorial(2 * i) for i in range(8)]


LIMIT = 20 * 2**20

VMEM = pl.BlockSpec(memory_space=pltpu.VMEM)
SMEM = pl.BlockSpec(memory_space=pltpu.SMEM)
GRANT = pltpu.CompilerParams(vmem_limit_bytes=LIMIT)


def tables(count):
    times = jnp.arange(TS, dtype=jnp.float32)[:, None]
    bins = (jnp.arange(count, dtype=jnp.int32) + band_start).astype(jnp.float32)[None, :]
    phase = 2.0 * jnp.pi * times * bins / TS
    return (jnp.cos(phase), jnp.sin(phase))


def contract_time(table, values):
    return jnp.einsum("tf,frk->trk", table, values, precision=highest)


def contract_back(table, values):
    return jnp.einsum("tf,trk->frk", table, values, precision=highest)


def time_gate(field, cos_table, sin_table, limits, complement):
    real_part = field[:, :, 0]
    imag_part = field[:, :, 1]
    time_real = contract_time(cos_table, real_part) - contract_time(sin_table, imag_part)
    time_imag = contract_time(sin_table, real_part) + contract_time(cos_table, imag_part)
    clock = jnp.arange(TS, dtype=jnp.int32)[:, None, None]
    window = (clock < limits[None]).astype(jnp.float32)
    if complement:
        window = 1.0 - window
    kept_real = window * time_real
    kept_imag = window * time_imag
    out_real = (contract_back(cos_table, kept_real) + contract_back(sin_table, kept_imag)) / TS
    out_imag = (contract_back(cos_table, kept_imag) - contract_back(sin_table, kept_real)) / TS
    return jnp.stack([out_real, out_imag], axis=2)


def combine(total, conjugate):
    if conjugate:
        out_real = total[:, 0, :, 0] + total[:, 1, :, 1]
        out_imag = total[:, 0, :, 1] - total[:, 1, :, 0]
    else:
        out_real = total[:, 0, :, 0] - total[:, 1, :, 1]
        out_imag = total[:, 0, :, 1] + total[:, 1, :, 0]
    return jnp.stack([out_real, out_imag], axis=2)


def per_device_general(reflection, starts, focusing, residual, direction, gradient):
    local_rows = reflection.shape[2]
    positions = reflection.shape[3]
    groups = lax.axis_size("freq")
    position = lax.axis_index("freq")
    cos_table, sin_table = tables(reflection.shape[0] * groups)

    def gate(field, complement):
        spread = lax.all_to_all(field, "freq", split_axis=1, concat_axis=0, tiled=True)
        share = local_rows // groups
        limits = lax.dynamic_slice_in_dim(starts, position * share, share, 0)
        gated_part = time_gate(spread, cos_table, sin_table, limits, complement)
        return lax.all_to_all(gated_part, "freq", split_axis=0, concat_axis=1, tiled=True)

    def accumulate(piece):
        return jnp.einsum("fpnm,fmqk->fpnqk", reflection, piece, preferred_element_type=jnp.float32)

    direction_low = direction.astype(jnp.bfloat16)
    focusing_low = focusing.astype(jnp.bfloat16)
    aimed_total = accumulate(lax.all_gather(direction_low, "rcv", axis=1, tiled=True))
    direction_image = combine(aimed_total, False)
    gamma = lax.psum(jnp.sum(gradient * gradient), ("freq", "rcv"))
    image = gate(direction_image, False)
    curvature = lax.psum(jnp.sum(image * image), ("freq", "rcv"))
    alpha = gamma / (curvature + tiny)
    new_focusing = focusing + alpha * direction
    new_residual = residual - alpha * image
    gated = gate(new_residual, False).astype(jnp.bfloat16)
    total = accumulate(lax.all_gather(gated, "rcv", axis=1, tiled=True))
    new_gradient = combine(total, True)
    new_gamma = lax.psum(jnp.sum(new_gradient * new_gradient), ("freq", "rcv"))
    new_direction = new_gradient + new_gamma / (gamma + tiny) * direction
    focus_total = accumulate(lax.all_gather(focusing_low, "rcv", axis=1, tiled=True))
    focusing_image = combine(focus_total, False)
    green_field = gate(focusing_image + alpha * direction_image, True)
    corr_real = jnp.sum(
        green_field[:, :, 0] * new_focusing[:, :, 0] + green_field[:, :, 1] * new_focusing[:, :, 1],
        axis=1,
    )
    corr_imag = jnp.sum(
        green_field[:, :, 1] * new_focusing[:, :, 0] - green_field[:, :, 0] * new_focusing[:, :, 1],
        axis=1,
    )
    partial_corr = jnp.stack([corr_real, corr_imag], axis=1)
    focal_correlation = lax.psum(partial_corr, "rcv") / math.sqrt(positions)
    return (new_focusing, new_residual, new_direction, green_field, focal_correlation)


def split_row(x, odd):
    main = x.shape[-1] - HALF
    return (x[:, HALF:], x[:, :HALF]) if odd else (x[:, :main], x[:, main:])


def pack(real, imag, odd):
    (r_main, r_tail), (i_main, i_tail) = split_row(real, odd), split_row(imag, odd)
    return jnp.concatenate([r_main, i_main, jnp.concatenate([r_tail, i_tail], axis=1)], axis=1)


def unpack(row, plane, odd):
    main = row.shape[-1] // 2 - HALF
    tail = 2 * main + plane * HALF
    parts = [row[:, plane * main : (plane + 1) * main], row[:, tail : tail + HALF]]
    return jnp.concatenate(parts[::-1] if odd else parts, axis=1)


def by_parity(pos_ref, body):
    for odd in range(2):
        pl.when(pos_ref[1] == odd)(lambda odd=odd: body(odd))


def cost(flops, size):
    return pl.CostEstimate(flops=int(flops), bytes_accessed=int(size), transcendentals=0)


def prep_low_kernel(pos_ref, x_ref, o_ref):
    def body(odd):
        for f in range(x_ref.shape[0]):
            o_ref[f] = pack(x_ref[f, 0], x_ref[f, 1], odd).astype(jnp.bfloat16)

    by_parity(pos_ref, body)


def prep_low(pos, x):
    loc, _, k, n = x.shape
    return pl.pallas_call(
        prep_low_kernel,
        out_shape=jax.ShapeDtypeStruct((loc, k, 2 * n), jnp.bfloat16),
        in_specs=[SMEM, VMEM],
        out_specs=VMEM,
        cost_estimate=cost(x.size, 6 * x.size),
        compiler_params=GRANT,
        name="prep_low",
    )(pos, x)


def share_of(me, p, groups):
    if groups & (groups - 1) == 0:
        return me ^ p
    return lax.rem(p - me + groups, groups)


def prep_shares_kernel(groups, pos_ref, x_ref, g_ref, *o_refs):
    me = pos_ref[0]
    ks = x_ref.shape[2] // groups

    def body(odd):
        for p in range(groups):
            at = pl.multiple_of(share_of(me, p, groups) * ks, ks)
            for f in range(x_ref.shape[0]):
                real, imag = x_ref[f, 0, pl.ds(at, ks), :], x_ref[f, 1, pl.ds(at, ks), :]
                o_refs[p][f] = pack(real, imag, odd)

    by_parity(pos_ref, body)
    total = jnp.zeros((8, g_ref.shape[3]), jnp.float32)
    for f in range(g_ref.shape[0]):
        for c in range(2):
            for r in range(0, g_ref.shape[2], 8):
                v = g_ref[f, c, r : r + 8, :]
                total = total + v * v
    o_refs[groups][...] = lane_fold(jnp.sum(total, axis=0, keepdims=True))


def lane_fold(row, width=LANES):
    out = jnp.sum(row, axis=1, keepdims=True)
    lane = lax.broadcasted_iota(jnp.int32, (1, width), 1)
    return jnp.where(lane == 0, out, 0.0)


def prep_shares(pos, x, g, groups):
    loc, _, k, n = x.shape
    outs = [jax.ShapeDtypeStruct((loc, k // groups, 2 * n), jnp.float32)] * groups
    return pl.pallas_call(
        lambda *refs: prep_shares_kernel(groups, *refs),
        out_shape=outs + [jax.ShapeDtypeStruct((1, LANES), jnp.float32)],
        in_specs=[SMEM, VMEM, VMEM],
        out_specs=[VMEM] * (groups + 1),
        cost_estimate=cost(3 * x.size, 12 * x.size),
        compiler_params=GRANT,
        name="prep_shares",
    )(pos, x, g)


def product_kernel(groups, count, back, pos_ref, r_ref, *refs):
    blocks, refs = refs[: 2 * count], refs[2 * count :]
    v_scr, acc = refs[-2:]
    loc, kc, wide = blocks[0].shape
    rows = r_ref.shape[2]
    main = wide // 2 - HALF
    me = pos_ref[0]

    def load(f, odd):
        for b in range(count):
            even = blocks[2 * b + odd]
            other = blocks[2 * b + 1 - odd]
            at = pos_ref[2 + b] * wide
            for c in range(2):
                here = slice(c * kc, (c + 1) * kc)
                half = slice(2 * main + c * HALF, 2 * main + (c + 1) * HALF)
                lanes = lambda shift, size: pl.ds(pl.multiple_of(at + shift, LANES), size)
                v_scr[here, lanes(0, main)] = even[f, :, c * main : (c + 1) * main]
                middle = [even[f, :, half], other[f, :, half]]
                v_scr[here, lanes(main, LANES)] = jnp.concatenate(middle, axis=1)
                v_scr[here, lanes(main + LANES, main)] = other[f, :, c * main : (c + 1) * main]

    def shares(f, odd):
        ks = kc // groups
        for p in range(groups):
            at = pl.multiple_of(share_of(me, p, groups) * ks, ks)
            real = acc[pl.ds(at, ks), :rows] - acc[pl.ds(at + kc, ks), rows:]
            imag = acc[pl.ds(at + kc, ks), :rows] + acc[pl.ds(at, ks), rows:]
            refs[p][f] = pack(real, imag, odd)

    dims = (((1,), (1,)), ((), ()))
    total = 0.0
    for f in range(loc):
        by_parity(pos_ref, lambda odd: load(f, odd))
        both = r_ref[f].reshape(2 * rows, r_ref.shape[3])
        acc[...] = lax.dot_general(v_scr[...], both, dims, preferred_element_type=jnp.float32)
        if not back:
            by_parity(pos_ref, lambda odd: shares(f, odd))
        else:
            real = acc[:kc, :rows] + acc[kc:, rows:]
            imag = acc[kc:, :rows] - acc[:kc, rows:]
            refs[0][f, 0] = real
            refs[0][f, 1] = imag
            total = total + jnp.sum(real * real + imag * imag, axis=0, keepdims=True)
    if back:
        refs[1][...] = lane_fold(total)


def product(pos, reflection, blocks, groups, back=False):
    loc, _, rows, cols = reflection.shape
    kc, wide = blocks[0].shape[1:]
    count = len(blocks) // 2
    if not back:
        out_shape = [jax.ShapeDtypeStruct((loc, kc // groups, wide), jnp.float32)] * groups
    else:
        out_shape = [
            jax.ShapeDtypeStruct((loc, 2, kc, rows), jnp.float32),
            jax.ShapeDtypeStruct((1, LANES), jnp.float32),
        ]
    return pl.pallas_call(
        lambda *refs: product_kernel(groups, count, back, *refs),
        in_specs=[SMEM] + [VMEM] * (1 + 2 * count),
        out_specs=[VMEM] * len(out_shape),
        scratch_shapes=[
            pltpu.VMEM((2 * kc, cols), jnp.bfloat16),
            pltpu.VMEM((2 * kc, 2 * rows), jnp.float32),
        ],
        out_shape=out_shape,
        cost_estimate=cost(8 * loc * rows * cols * kc, 2 * reflection.size + 4 * loc * kc * cols),
        compiler_params=GRANT,
        name="product_back" if back else "product",
    )(pos, reflection, *blocks)


def turn_of(limit):
    x = (limit - TS / 2) * (math.pi / TS)
    y = x * x
    sine = jnp.full_like(y, SINE[-1])
    for v in SINE[-2::-1]:
        sine = sine * y + v
    sine = sine * x
    cosine = jnp.full_like(y, COSINE[-1])
    for v in COSINE[-2::-1]:
        cosine = cosine * y + v
    return 2.0 * sine * sine - 1.0, -2.0 * sine * cosine


def gate_weights(limit, count):
    c1, s1 = turn_of(limit)
    real = [limit * (1.0 / TS)]
    imag = [None]
    c, s = c1, s1
    for d in range(1, count):
        half_cot = 0.5 / math.tan(math.pi * d / TS)
        rest = 1.0 - c
        real.append((0.5 * rest + half_cot * s) * (1.0 / TS))
        imag.append((half_cot * rest - 0.5 * s) * (1.0 / TS))
        c, s = c * c1 - s * s1, s * c1 + c * s1
    return real, imag


def gate_pair(real, imag, ur, ui):
    count = len(ur)
    out_r, out_i = [], []
    for j in range(count):
        r = real[0] * ur[j]
        i = real[0] * ui[j]
        for m in range(count):
            d = abs(m - j)
            if m > j:
                r = r + real[d] * ur[m] - imag[d] * ui[m]
                i = i + real[d] * ui[m] + imag[d] * ur[m]
            elif m < j:
                r = r + real[d] * ur[m] + imag[d] * ui[m]
                i = i + real[d] * ui[m] - imag[d] * ur[m]
        out_r.append(r)
        out_i.append(i)
    return out_r, out_i


def gate_tail(real, signed, u):
    count = len(u)
    w = [pltpu.roll(v, HALF, 1) for v in u]
    outs = []
    for j in range(count):
        r = real[0] * u[j]
        for m in range(count):
            d = abs(m - j)
            if m > j:
                r = r + real[d] * u[m] + signed[d] * w[m]
            elif m < j:
                r = r + real[d] * u[m] - signed[d] * w[m]
        outs.append(r)
    return outs


def gate_kernel(groups, squares, mixed, pos_ref, s_ref, *refs):
    if squares:
        row_ref, refs = refs[0], refs[1:]
    if mixed:
        t_ref, bases, refs = refs[0], refs[1 : 1 + groups], refs[1 + groups :]
    ins = refs[:groups]
    outs = refs[groups : 2 * groups]
    rest = refs[2 * groups :]
    if squares:
        sum_ref, acc = rest[0], rest[1]
        rest = rest[2:]
        acc[...] = jnp.zeros_like(acc)
    u_scr, o_scr, lim_scr = rest
    me = pos_ref[0]
    loc, ks, wide = ins[0].shape
    count = groups * loc
    main = wide // 2 - HALF
    at = pl.multiple_of(me * ks, ks)
    lim = jnp.clip(s_ref[pl.ds(at, ks), :], 0, TS).astype(jnp.float32)

    def place(odd):
        whole, ends = split_row(lim, odd)
        lim_scr[:, :main] = whole
        lim_scr[:, main:] = jnp.concatenate([ends, ends], axis=1)

    by_parity(pos_ref, place)
    for p in range(groups):
        base = share_of(me, p, groups) * loc
        for f in range(loc):
            u_scr[base + f] = ins[p][f]

    def tile(i, carry):
        rows = pl.ds(pl.multiple_of(i * 8, 8), 8)
        for t in range(main // LANES + 1):
            real, imag = gate_weights(lim_scr[rows, t * LANES : (t + 1) * LANES], count)
            if t * LANES < main:
                re_at = slice(t * LANES, (t + 1) * LANES)
                im_at = slice(main + t * LANES, main + (t + 1) * LANES)
                ur = [u_scr[j, rows, re_at] for j in range(count)]
                ui = [u_scr[j, rows, im_at] for j in range(count)]
                out_r, out_i = gate_pair(real, imag, ur, ui)
                for j in range(count):
                    o_scr[j, rows, re_at] = out_r[j]
                    o_scr[j, rows, im_at] = out_i[j]
                    if squares:
                        acc[...] += out_r[j] * out_r[j] + out_i[j] * out_i[j]
            else:
                ends = slice(2 * main, 2 * main + LANES)
                lane = lax.broadcasted_iota(jnp.int32, (8, LANES), 1)
                sign = jnp.where(lane < HALF, -1.0, 1.0)
                signed = [None] + [v * sign for v in imag[1:]]
                out = gate_tail(real, signed, [u_scr[j, rows, ends] for j in range(count)])
                for j in range(count):
                    o_scr[j, rows, ends] = out[j]
                    if squares:
                        acc[...] += out[j] * out[j]
        return carry

    lax.fori_loop(0, ks // 8, tile, 0)
    for p in range(groups):
        base = share_of(me, p, groups) * loc
        for f in range(loc):
            if mixed:
                mix = bases[p][f] - alpha_of(t_ref)[0] * o_scr[base + f]
                outs[p][f] = mix.astype(jnp.bfloat16)
            else:
                outs[p][f] = o_scr[base + f]
    if squares:
        mine = lane_fold(jnp.sum(acc[...], axis=0, keepdims=True))
        both = jnp.concatenate([mine, row_ref[...]], axis=0)
        sum_ref[...] = jnp.broadcast_to(both[None], sum_ref.shape)


def gate(pos, limits, shares, groups, row=None, devices=0, sums=None, bases=()):
    squares = row is not None
    loc, ks, wide = shares[0].shape
    kind = jnp.bfloat16 if bases else jnp.float32
    out_shape = [jax.ShapeDtypeStruct((loc, ks, wide), kind)] * groups
    scratch = []
    more = []
    if squares:
        out_shape = out_shape + [jax.ShapeDtypeStruct((devices, 2, LANES), jnp.float32)]
        scratch = [pltpu.VMEM((8, LANES), jnp.float32)]
        more = [row]
    if bases:
        more = [sums, *bases]
    scratch = scratch + [
        pltpu.VMEM((groups * loc, ks, wide), jnp.float32),
        pltpu.VMEM((groups * loc, ks, wide), jnp.float32),
        pltpu.VMEM((ks, wide // 2 + HALF), jnp.float32),
    ]
    size = groups * loc * ks * wide
    return pl.pallas_call(
        lambda *refs: gate_kernel(groups, squares, bool(bases), *refs),
        out_shape=out_shape,
        in_specs=[SMEM, VMEM] + [VMEM] * (groups + len(more)),
        out_specs=[VMEM] * len(out_shape),
        scratch_shapes=scratch,
        cost_estimate=cost(40 * size, 8 * size),
        compiler_params=GRANT,
        name="gate_sum" if squares else "gate_mix" if bases else "gate",
    )(pos, limits, *more, *shares)


def alpha_of(t_ref):
    gamma = jnp.sum(t_ref[:, 1, :])
    curvature = jnp.sum(t_ref[:, 0, :])
    return gamma / (curvature + tiny), gamma


def join_kernel(groups, pos_ref, *refs):
    me = pos_ref[0]
    ks = refs[0].shape[1]
    for p in range(groups):
        at = pl.multiple_of(share_of(me, p, groups) * ks, ks)
        for f in range(refs[p].shape[0]):
            refs[groups][f, pl.ds(at, ks), :] = refs[p][f]


def join(pos, shares, groups):
    loc, ks, wide = shares[0].shape
    return pl.pallas_call(
        lambda *refs: join_kernel(groups, *refs),
        out_shape=jax.ShapeDtypeStruct((loc, groups * ks, wide), shares[0].dtype),
        in_specs=[SMEM] + [VMEM] * groups,
        out_specs=VMEM,
        cost_estimate=cost(0, 4 * groups * shares[0].size),
        compiler_params=GRANT,
        name="join",
    )(pos, *shares)


def update_kernel(groups, pos_ref, t_ref, res_ref, foc_ref, dir_ref, *refs):
    image = refs[:groups]
    nres_ref, nfoc_ref = refs[groups:]
    alpha, _ = alpha_of(t_ref)
    me = pos_ref[0]
    loc, ks, _ = image[0].shape
    nfoc_ref[...] = foc_ref[...] + alpha * dir_ref[...]

    def body(odd):
        for p in range(groups):
            rows = pl.ds(pl.multiple_of(share_of(me, p, groups) * ks, ks), ks)
            for f in range(loc):
                for c in range(2):
                    seen = unpack(image[p][f], c, odd)
                    nres_ref[f, c, rows, :] = res_ref[f, c, rows, :] - alpha * seen

    by_parity(pos_ref, body)


def update(pos, sums, residual, focusing, direction, image, groups):
    size = residual.size
    return pl.pallas_call(
        lambda *refs: update_kernel(groups, *refs),
        out_shape=[jax.ShapeDtypeStruct(residual.shape, jnp.float32)] * 2,
        in_specs=[SMEM] + [VMEM] * (4 + groups),
        out_specs=[VMEM] * 2,
        cost_estimate=cost(4 * size, 24 * size),
        compiler_params=GRANT,
        name="update",
    )(pos, sums, residual, focusing, direction, *image)


def green_kernel(groups, pos_ref, t_ref, nfoc_ref, row_ref, *refs):
    image, kept, di, fi = [refs[i * groups : (i + 1) * groups] for i in range(4)]
    green_ref, sent_ref, corr_scr = refs[4 * groups :]
    alpha, _ = alpha_of(t_ref)
    me = pos_ref[0]
    loc, ks, _ = di[0].shape

    def body(odd):
        for p in range(groups):
            rows = pl.ds(pl.multiple_of(share_of(me, p, groups) * ks, ks), ks)
            for f in range(loc):
                row = (fi[p][f] - kept[p][f]) + alpha * (di[p][f] - image[p][f])
                for c in range(2):
                    green_ref[f, c, rows, :] = unpack(row, c, odd)

    by_parity(pos_ref, body)
    ones = jnp.ones((8, nfoc_ref.shape[3]), jnp.float32)
    dims = (((1,), (1,)), ((), ()))
    for f in range(loc):
        gr, gi, fr, fm = green_ref[f, 0], green_ref[f, 1], nfoc_ref[f, 0], nfoc_ref[f, 1]
        for c, value in enumerate((gr * fr + gi * fm, gi * fr - gr * fm)):
            line = lax.dot_general(ones, value, dims, precision=highest, preferred_element_type=jnp.float32)
            corr_scr[2 * f + c : 2 * f + c + 1, :] = line[:1]
    total = jnp.broadcast_to(row_ref[:, :HALF], (2 * loc, HALF))
    ends = jnp.concatenate([corr_scr[:, LANES:], total], axis=1)
    table = jnp.concatenate([corr_scr[:, :LANES], ends], axis=0)
    sent_ref[...] = jnp.broadcast_to(table[None], sent_ref.shape)


def green(pos, sums, new_focusing, row, image, kept, di, fi, groups):
    loc, _, k, _ = new_focusing.shape
    size = new_focusing.size
    return pl.pallas_call(
        lambda *refs: green_kernel(groups, *refs),
        out_shape=[
            jax.ShapeDtypeStruct(new_focusing.shape, jnp.float32),
            jax.ShapeDtypeStruct((sums.shape[0], 4 * loc, LANES), jnp.float32),
        ],
        in_specs=[SMEM] + [VMEM] * (3 + 4 * groups),
        out_specs=[VMEM] * 2,
        scratch_shapes=[pltpu.VMEM((2 * loc, k), jnp.float32)],
        cost_estimate=cost(12 * size, 24 * size),
        compiler_params=GRANT,
        name="green",
    )(pos, sums, new_focusing, row, *image, *kept, *di, *fi)


def turn(pos, sums, new_sums, new_gradient, direction, ranks):
    loc, _, points, n = direction.shape
    size = direction.size
    lines = 2 * loc
    scale = 1.0 / math.sqrt(n * ranks)

    def body(pos_ref, t_ref, g_ref, new_ref, dir_ref, out_ref, corr_ref):
        _, gamma = alpha_of(t_ref)
        beta = jnp.sum(g_ref[:, lines, HALF:]) / (gamma + tiny)
        out_ref[...] = new_ref[...] + beta * dir_ref[...]
        total = jnp.zeros((2 * lines, LANES), jnp.float32)
        for r in range(ranks):
            total = total + g_ref[pos_ref[0] * ranks + r]
        total = jnp.concatenate([total[:lines], total[lines:, :HALF]], axis=1) * scale
        for f in range(loc):
            corr_ref[f] = total[2 * f : 2 * f + 2]

    return pl.pallas_call(
        body,
        in_specs=[SMEM] + [VMEM] * 4,
        out_specs=[VMEM] * 2,
        out_shape=[
            jax.ShapeDtypeStruct(direction.shape, jnp.float32),
            jax.ShapeDtypeStruct((loc, 2, points), jnp.float32),
        ],
        cost_estimate=cost(2 * size, 12 * size),
        compiler_params=GRANT,
        name="turn",
    )(pos, sums, new_sums, new_gradient, direction)


def exchange(shares, groups):
    out = [shares[0]]
    for p in range(1, groups):
        pairs = [(m, share_of(m, p, groups) if groups & (groups - 1) == 0 else (p - m) % groups) for m in range(groups)]
        out.append(lax.ppermute(shares[p], "freq", pairs))
    return out


def side(deep, pick):
    pairs = []
    for z in range(deep):
        for y in range(2):
            to = pick(z, y)
            if to is not None:
                pairs.append((z * 2 + y, to[0] * 2 + to[1]))
    return pairs


def spread(own, mid):
    swap = side(4, lambda z, y: (z, 1 - y))
    near = side(4, lambda z, y: (z ^ 1, y))
    centre = side(4, lambda z, y: (3 - z, y) if z in (1, 2) else None)
    outward = side(4, lambda z, y: (0 if z == 1 else 3, y) if z in (1, 2) else None)

    def move(v, pairs):
        return lax.ppermute(v, "rcv", pairs)

    n1 = move(own, near)
    c1 = move(own, centre)
    y0 = move(own, swap)
    c2 = move(n1, centre)
    y1 = move(n1, swap)
    o1 = move(c1, outward)
    before = yield
    if before is not None:
        c2, o1, before = lax.optimization_barrier((c2, o1, before))
    yield before
    m1 = jnp.where(mid, c1, o1)
    y2 = move(m1, swap)
    o2 = move(c2, outward)
    m2 = jnp.where(mid, c2, o2)
    y3 = move(m2, swap)
    yield [own, y0, n1, y1, m1, y2, m2, y3]


def spread_all(own, mid):
    return list(spread(own, mid))[-1]


def total_over_all(sent):
    return lax.all_to_all(sent, ("freq", "rcv"), split_axis=0, concat_axis=0, tiled=True)


def per_device(reflection, starts, focusing, residual, direction, gradient):
    groups = lax.axis_size("freq")
    ranks = lax.axis_size("rcv")
    lay = lambda v: jnp.transpose(v, (0, 2, 3, 1))
    focusing, residual, direction, gradient = map(lay, (focusing, residual, direction, gradient))
    limits = jnp.transpose(starts, (1, 0))
    me = lax.axis_index("freq")
    rank = lax.axis_index("rcv")
    z, y = rank // 2, rank % 2
    mid = (z == 1) | (z == 2)
    far1 = jnp.where(z < 2, 2, 1)
    far2 = jnp.where(z < 2, 3, 0)
    pos = jnp.stack([me, y, z, z ^ 1, far1, far2]).astype(jnp.int32)

    blocks = spread_all(prep_low(pos, direction), mid)
    *res_shares, gamma_row = prep_shares(pos, residual, gradient, groups)
    res_there = exchange(res_shares, groups)
    kept_res = gate(pos, limits, res_there, groups)
    foc_own = prep_low(pos, focusing)
    aside = spread(foc_own, mid)
    next(aside)
    di = product(pos, reflection, blocks, groups)
    *image_there, sent = gate(pos, limits, exchange(di, groups), groups, gamma_row, groups * ranks)
    sums = total_over_all(sent)
    sums = aside.send(sums)
    foc = next(aside)
    gated_there = gate(pos, limits, image_there, groups, sums=sums, bases=kept_res)
    gated = join(pos, exchange(gated_there, groups), groups)
    blocks = spread_all(gated, mid)

    fi = product(pos, reflection, foc, groups)
    kept = gate(pos, limits, exchange(fi, groups), groups)
    kept = exchange(kept, groups)
    image = exchange(image_there, groups)
    new_residual, new_focusing = update(
        pos, sums, residual, focusing, direction, image, groups
    )
    new_gradient, row = product(pos, reflection, blocks, groups, True)
    green_field, new_sent = green(pos, sums, new_focusing, row, image, kept, di, fi, groups)
    new_sums = total_over_all(new_sent)
    new_direction, focal_correlation = turn(pos, sums, new_sums, new_gradient, direction, ranks)
    back = lambda v: jnp.transpose(v, (0, 3, 1, 2))
    return (back(new_focusing), back(new_residual), back(new_direction), back(green_field), focal_correlation)


def chosen(mesh):
    def run(reflection, starts, *fields):
        rows, points = starts.shape
        suits = (
            mesh.shape["rcv"] == 8
            and rows % LANES == HALF
            and rows > LANES
            and points % (16 * mesh.shape["freq"]) == 0
            and points == LANES + HALF
        )
        plan = per_device if suits else per_device_general
        return plan(reflection, starts, *fields)

    return run


def solution(mesh):
    return jax.shard_map(
        chosen(mesh),
        mesh=mesh,
        in_specs=(
            P("freq", None, "rcv", None),
            P("rcv", None),
            P("freq", "rcv", None, None),
            P("freq", "rcv", None, None),
            P("freq", "rcv", None, None),
            P("freq", "rcv", None, None),
        ),
        out_specs=(
            P("freq", "rcv", None, None),
            P("freq", "rcv", None, None),
            P("freq", "rcv", None, None),
            P("freq", "rcv", None, None),
            P("freq", None, None),
        ),
        check_vma=False,
    )
```

```python
import math

import jax
import jax.numpy as jnp
from jax import lax
from jax.experimental import pallas as pl
from jax.experimental.pallas import tpu as pltpu
from jax.sharding import PartitionSpec as P


TS = 64
band_start = 5
tiny = 1e-06
highest = lax.Precision.HIGHEST
LANES = 128
HALF = 64
SINE = [(-1.0) ** i / math.factorial(2 * i + 1) for i in range(7)]
COSINE = [(-1.0) ** i / math.factorial(2 * i) for i in range(8)]


LIMIT = 20 * 2**20

VMEM = pl.BlockSpec(memory_space=pltpu.VMEM)
SMEM = pl.BlockSpec(memory_space=pltpu.SMEM)
GRANT = pltpu.CompilerParams(vmem_limit_bytes=LIMIT)


def tables(count):
    times = jnp.arange(TS, dtype=jnp.float32)[:, None]
    bins = (jnp.arange(count, dtype=jnp.int32) + band_start).astype(jnp.float32)[None, :]
    phase = 2.0 * jnp.pi * times * bins / TS
    return (jnp.cos(phase), jnp.sin(phase))


def contract_time(table, values):
    return jnp.einsum("tf,frk->trk", table, values, precision=highest)


def contract_back(table, values):
    return jnp.einsum("tf,trk->frk", table, values, precision=highest)


def time_gate(field, cos_table, sin_table, limits, complement):
    real_part = field[:, :, 0]
    imag_part = field[:, :, 1]
    time_real = contract_time(cos_table, real_part) - contract_time(sin_table, imag_part)
    time_imag = contract_time(sin_table, real_part) + contract_time(cos_table, imag_part)
    clock = jnp.arange(TS, dtype=jnp.int32)[:, None, None]
    window = (clock < limits[None]).astype(jnp.float32)
    if complement:
        window = 1.0 - window
    kept_real = window * time_real
    kept_imag = window * time_imag
    out_real = (contract_back(cos_table, kept_real) + contract_back(sin_table, kept_imag)) / TS
    out_imag = (contract_back(cos_table, kept_imag) - contract_back(sin_table, kept_real)) / TS
    return jnp.stack([out_real, out_imag], axis=2)


def combine(total, conjugate):
    if conjugate:
        out_real = total[:, 0, :, 0] + total[:, 1, :, 1]
        out_imag = total[:, 0, :, 1] - total[:, 1, :, 0]
    else:
        out_real = total[:, 0, :, 0] - total[:, 1, :, 1]
        out_imag = total[:, 0, :, 1] + total[:, 1, :, 0]
    return jnp.stack([out_real, out_imag], axis=2)


def per_device_general(reflection, starts, focusing, residual, direction, gradient):
    local_rows = reflection.shape[2]
    positions = reflection.shape[3]
    groups = lax.axis_size("freq")
    position = lax.axis_index("freq")
    cos_table, sin_table = tables(reflection.shape[0] * groups)

    def gate(field, complement):
        spread = lax.all_to_all(field, "freq", split_axis=1, concat_axis=0, tiled=True)
        share = local_rows // groups
        limits = lax.dynamic_slice_in_dim(starts, position * share, share, 0)
        gated_part = time_gate(spread, cos_table, sin_table, limits, complement)
        return lax.all_to_all(gated_part, "freq", split_axis=0, concat_axis=1, tiled=True)

    def accumulate(piece):
        return jnp.einsum("fpnm,fmqk->fpnqk", reflection, piece, preferred_element_type=jnp.float32)

    direction_low = direction.astype(jnp.bfloat16)
    focusing_low = focusing.astype(jnp.bfloat16)
    aimed_total = accumulate(lax.all_gather(direction_low, "rcv", axis=1, tiled=True))
    direction_image = combine(aimed_total, False)
    gamma = lax.psum(jnp.sum(gradient * gradient), ("freq", "rcv"))
    image = gate(direction_image, False)
    curvature = lax.psum(jnp.sum(image * image), ("freq", "rcv"))
    alpha = gamma / (curvature + tiny)
    new_focusing = focusing + alpha * direction
    new_residual = residual - alpha * image
    gated = gate(new_residual, False).astype(jnp.bfloat16)
    total = accumulate(lax.all_gather(gated, "rcv", axis=1, tiled=True))
    new_gradient = combine(total, True)
    new_gamma = lax.psum(jnp.sum(new_gradient * new_gradient), ("freq", "rcv"))
    new_direction = new_gradient + new_gamma / (gamma + tiny) * direction
    focus_total = accumulate(lax.all_gather(focusing_low, "rcv", axis=1, tiled=True))
    focusing_image = combine(focus_total, False)
    green_field = gate(focusing_image + alpha * direction_image, True)
    corr_real = jnp.sum(
        green_field[:, :, 0] * new_focusing[:, :, 0] + green_field[:, :, 1] * new_focusing[:, :, 1],
        axis=1,
    )
    corr_imag = jnp.sum(
        green_field[:, :, 1] * new_focusing[:, :, 0] - green_field[:, :, 0] * new_focusing[:, :, 1],
        axis=1,
    )
    partial_corr = jnp.stack([corr_real, corr_imag], axis=1)
    focal_correlation = lax.psum(partial_corr, "rcv") / math.sqrt(positions)
    return (new_focusing, new_residual, new_direction, green_field, focal_correlation)


def split_row(x, odd):
    main = x.shape[-1] - HALF
    return (x[:, HALF:], x[:, :HALF]) if odd else (x[:, :main], x[:, main:])


def pack(real, imag, odd):
    (r_main, r_tail), (i_main, i_tail) = split_row(real, odd), split_row(imag, odd)
    return jnp.concatenate([r_main, i_main, jnp.concatenate([r_tail, i_tail], axis=1)], axis=1)


def unpack(row, plane, odd):
    main = row.shape[-1] // 2 - HALF
    tail = 2 * main + plane * HALF
    parts = [row[:, plane * main : (plane + 1) * main], row[:, tail : tail + HALF]]
    return jnp.concatenate(parts[::-1] if odd else parts, axis=1)


def by_parity(pos_ref, body):
    for odd in range(2):
        pl.when(pos_ref[1] == odd)(lambda odd=odd: body(odd))


def cost(flops, size):
    return pl.CostEstimate(flops=int(flops), bytes_accessed=int(size), transcendentals=0)


def prep_low_kernel(pos_ref, x_ref, o_ref):
    def body(odd):
        for f in range(x_ref.shape[0]):
            o_ref[f] = pack(x_ref[f, 0], x_ref[f, 1], odd).astype(jnp.bfloat16)

    by_parity(pos_ref, body)


def prep_low(pos, x):
    loc, _, k, n = x.shape
    return pl.pallas_call(
        prep_low_kernel,
        out_shape=jax.ShapeDtypeStruct((loc, k, 2 * n), jnp.bfloat16),
        in_specs=[SMEM, VMEM],
        out_specs=VMEM,
        cost_estimate=cost(x.size, 6 * x.size),
        compiler_params=GRANT,
        name="prep_low",
    )(pos, x)


def share_of(me, p, groups):
    if groups & (groups - 1) == 0:
        return me ^ p
    return lax.rem(p - me + groups, groups)


def prep_shares_kernel(groups, pos_ref, x_ref, g_ref, *o_refs):
    me = pos_ref[0]
    ks = x_ref.shape[2] // groups

    def body(odd):
        for p in range(groups):
            at = pl.multiple_of(share_of(me, p, groups) * ks, ks)
            for f in range(x_ref.shape[0]):
                real, imag = x_ref[f, 0, pl.ds(at, ks), :], x_ref[f, 1, pl.ds(at, ks), :]
                o_refs[p][f] = pack(real, imag, odd)

    by_parity(pos_ref, body)
    total = jnp.zeros((8, g_ref.shape[3]), jnp.float32)
    for f in range(g_ref.shape[0]):
        for c in range(2):
            for r in range(0, g_ref.shape[2], 8):
                v = g_ref[f, c, r : r + 8, :]
                total = total + v * v
    o_refs[groups][...] = lane_fold(jnp.sum(total, axis=0, keepdims=True))


def lane_fold(row, width=LANES):
    out = jnp.sum(row, axis=1, keepdims=True)
    lane = lax.broadcasted_iota(jnp.int32, (1, width), 1)
    return jnp.where(lane == 0, out, 0.0)


def prep_shares(pos, x, g, groups):
    loc, _, k, n = x.shape
    outs = [jax.ShapeDtypeStruct((loc, k // groups, 2 * n), jnp.float32)] * groups
    return pl.pallas_call(
        lambda *refs: prep_shares_kernel(groups, *refs),
        out_shape=outs + [jax.ShapeDtypeStruct((1, LANES), jnp.float32)],
        in_specs=[SMEM, VMEM, VMEM],
        out_specs=[VMEM] * (groups + 1),
        cost_estimate=cost(3 * x.size, 12 * x.size),
        compiler_params=GRANT,
        name="prep_shares",
    )(pos, x, g)


def product_kernel(groups, count, back, pos_ref, r_ref, *refs):
    blocks, refs = refs[: 2 * count], refs[2 * count :]
    v_scr, acc = refs[-2:]
    loc, kc, wide = blocks[0].shape
    rows = r_ref.shape[2]
    main = wide // 2 - HALF
    me = pos_ref[0]

    def load(f, odd):
        for b in range(count):
            even = blocks[2 * b + odd]
            other = blocks[2 * b + 1 - odd]
            at = pos_ref[2 + b] * wide
            for c in range(2):
                here = slice(c * kc, (c + 1) * kc)
                half = slice(2 * main + c * HALF, 2 * main + (c + 1) * HALF)
                lanes = lambda shift, size: pl.ds(pl.multiple_of(at + shift, LANES), size)
                v_scr[here, lanes(0, main)] = even[f, :, c * main : (c + 1) * main]
                middle = [even[f, :, half], other[f, :, half]]
                v_scr[here, lanes(main, LANES)] = jnp.concatenate(middle, axis=1)
                v_scr[here, lanes(main + LANES, main)] = other[f, :, c * main : (c + 1) * main]

    def shares(f, odd):
        ks = kc // groups
        for p in range(groups):
            at = pl.multiple_of(share_of(me, p, groups) * ks, ks)
            real = acc[pl.ds(at, ks), :rows] - acc[pl.ds(at + kc, ks), rows:]
            imag = acc[pl.ds(at + kc, ks), :rows] + acc[pl.ds(at, ks), rows:]
            refs[p][f] = pack(real, imag, odd)

    dims = (((1,), (1,)), ((), ()))
    total = 0.0
    for f in range(loc):
        by_parity(pos_ref, lambda odd: load(f, odd))
        both = r_ref[f].reshape(2 * rows, r_ref.shape[3])
        acc[...] = lax.dot_general(v_scr[...], both, dims, preferred_element_type=jnp.float32)
        if not back:
            by_parity(pos_ref, lambda odd: shares(f, odd))
        else:
            real = acc[:kc, :rows] + acc[kc:, rows:]
            imag = acc[kc:, :rows] - acc[:kc, rows:]
            refs[0][f, 0] = real
            refs[0][f, 1] = imag
            total = total + jnp.sum(real * real + imag * imag, axis=0, keepdims=True)
    if back:
        refs[1][...] = lane_fold(total)


def product(pos, reflection, blocks, groups, back=False):
    loc, _, rows, cols = reflection.shape
    kc, wide = blocks[0].shape[1:]
    count = len(blocks) // 2
    if not back:
        out_shape = [jax.ShapeDtypeStruct((loc, kc // groups, wide), jnp.float32)] * groups
    else:
        out_shape = [
            jax.ShapeDtypeStruct((loc, 2, kc, rows), jnp.float32),
            jax.ShapeDtypeStruct((1, LANES), jnp.float32),
        ]
    return pl.pallas_call(
        lambda *refs: product_kernel(groups, count, back, *refs),
        in_specs=[SMEM] + [VMEM] * (1 + 2 * count),
        out_specs=[VMEM] * len(out_shape),
        scratch_shapes=[
            pltpu.VMEM((2 * kc, cols), jnp.bfloat16),
            pltpu.VMEM((2 * kc, 2 * rows), jnp.float32),
        ],
        out_shape=out_shape,
        cost_estimate=cost(8 * loc * rows * cols * kc, 2 * reflection.size + 4 * loc * kc * cols),
        compiler_params=GRANT,
        name="product_back" if back else "product",
    )(pos, reflection, *blocks)


def turn_of(limit):
    x = (limit - TS / 2) * (math.pi / TS)
    y = x * x
    sine = jnp.full_like(y, SINE[-1])
    for v in SINE[-2::-1]:
        sine = sine * y + v
    sine = sine * x
    cosine = jnp.full_like(y, COSINE[-1])
    for v in COSINE[-2::-1]:
        cosine = cosine * y + v
    return 2.0 * sine * sine - 1.0, -2.0 * sine * cosine


def gate_weights(limit, count):
    c1, s1 = turn_of(limit)
    real = [limit * (1.0 / TS)]
    imag = [None]
    c, s = c1, s1
    for d in range(1, count):
        half_cot = 0.5 / math.tan(math.pi * d / TS)
        rest = 1.0 - c
        real.append((0.5 * rest + half_cot * s) * (1.0 / TS))
        imag.append((half_cot * rest - 0.5 * s) * (1.0 / TS))
        c, s = c * c1 - s * s1, s * c1 + c * s1
    return real, imag


def gate_pair(real, imag, ur, ui):
    count = len(ur)
    out_r, out_i = [], []
    for j in range(count):
        r = real[0] * ur[j]
        i = real[0] * ui[j]
        for m in range(count):
            d = abs(m - j)
            if m > j:
                r = r + real[d] * ur[m] - imag[d] * ui[m]
                i = i + real[d] * ui[m] + imag[d] * ur[m]
            elif m < j:
                r = r + real[d] * ur[m] + imag[d] * ui[m]
                i = i + real[d] * ui[m] - imag[d] * ur[m]
        out_r.append(r)
        out_i.append(i)
    return out_r, out_i


def gate_tail(real, signed, u):
    count = len(u)
    w = [pltpu.roll(v, HALF, 1) for v in u]
    outs = []
    for j in range(count):
        r = real[0] * u[j]
        for m in range(count):
            d = abs(m - j)
            if m > j:
                r = r + real[d] * u[m] + signed[d] * w[m]
            elif m < j:
                r = r + real[d] * u[m] - signed[d] * w[m]
        outs.append(r)
    return outs


def gate_kernel(groups, squares, mixed, near, pos_ref, s_ref, *refs):
    refs = refs[near:]
    if squares:
        row_ref, refs = refs[0], refs[1:]
    if mixed:
        t_ref, bases, refs = refs[0], refs[1 : 1 + groups], refs[1 + groups :]
    ins = refs[:groups]
    outs = refs[groups : 2 * groups]
    rest = refs[2 * groups :]
    if squares:
        sum_ref, acc = rest[0], rest[1]
        rest = rest[2:]
        acc[...] = jnp.zeros_like(acc)
    u_scr, o_scr, lim_scr = rest
    me = pos_ref[0]
    loc, ks, wide = ins[0].shape
    count = groups * loc
    main = wide // 2 - HALF
    at = pl.multiple_of(me * ks, ks)
    lim = jnp.clip(s_ref[pl.ds(at, ks), :], 0, TS).astype(jnp.float32)

    def place(odd):
        whole, ends = split_row(lim, odd)
        lim_scr[:, :main] = whole
        lim_scr[:, main:] = jnp.concatenate([ends, ends], axis=1)

    by_parity(pos_ref, place)
    for p in range(groups):
        base = share_of(me, p, groups) * loc
        for f in range(loc):
            u_scr[base + f] = ins[p][f]

    def tile(i, carry):
        rows = pl.ds(pl.multiple_of(i * 8, 8), 8)
        for t in range(main // LANES + 1):
            real, imag = gate_weights(lim_scr[rows, t * LANES : (t + 1) * LANES], count)
            if t * LANES < main:
                re_at = slice(t * LANES, (t + 1) * LANES)
                im_at = slice(main + t * LANES, main + (t + 1) * LANES)
                ur = [u_scr[j, rows, re_at] for j in range(count)]
                ui = [u_scr[j, rows, im_at] for j in range(count)]
                out_r, out_i = gate_pair(real, imag, ur, ui)
                for j in range(count):
                    o_scr[j, rows, re_at] = out_r[j]
                    o_scr[j, rows, im_at] = out_i[j]
                    if squares:
                        acc[...] += out_r[j] * out_r[j] + out_i[j] * out_i[j]
            else:
                ends = slice(2 * main, 2 * main + LANES)
                lane = lax.broadcasted_iota(jnp.int32, (8, LANES), 1)
                sign = jnp.where(lane < HALF, -1.0, 1.0)
                signed = [None] + [v * sign for v in imag[1:]]
                out = gate_tail(real, signed, [u_scr[j, rows, ends] for j in range(count)])
                for j in range(count):
                    o_scr[j, rows, ends] = out[j]
                    if squares:
                        acc[...] += out[j] * out[j]
        return carry

    lax.fori_loop(0, ks // 8, tile, 0)
    for p in range(groups):
        base = share_of(me, p, groups) * loc
        for f in range(loc):
            if mixed:
                mix = bases[p][f] - alpha_of(t_ref)[0] * o_scr[base + f]
                outs[p][f] = mix.astype(jnp.bfloat16)
            else:
                outs[p][f] = o_scr[base + f]
    if squares:
        mine = lane_fold(jnp.sum(acc[...], axis=0, keepdims=True))
        both = jnp.concatenate([mine, row_ref[...]], axis=0)
        sum_ref[...] = jnp.broadcast_to(both[None], sum_ref.shape)


def gate(pos, limits, shares, groups, row=None, devices=0, sums=None, bases=(), near=None):
    squares = row is not None
    loc, ks, wide = shares[0].shape
    kind = jnp.bfloat16 if bases else jnp.float32
    out_shape = [jax.ShapeDtypeStruct((loc, ks, wide), kind)] * groups
    scratch = []
    more = []
    if squares:
        out_shape = out_shape + [jax.ShapeDtypeStruct((devices, 2, LANES), jnp.float32)]
        scratch = [pltpu.VMEM((8, LANES), jnp.float32)]
        more = [row]
    if bases:
        more = [sums, *bases]
    if near is not None:
        more = [near]
    scratch = scratch + [
        pltpu.VMEM((groups * loc, ks, wide), jnp.float32),
        pltpu.VMEM((groups * loc, ks, wide), jnp.float32),
        pltpu.VMEM((ks, wide // 2 + HALF), jnp.float32),
    ]
    size = groups * loc * ks * wide
    return pl.pallas_call(
        lambda *refs: gate_kernel(groups, squares, bool(bases), near is not None, *refs),
        out_shape=out_shape,
        in_specs=[SMEM, VMEM] + [VMEM] * (groups + len(more)),
        out_specs=[VMEM] * len(out_shape),
        scratch_shapes=scratch,
        cost_estimate=cost(40 * size, 8 * size),
        compiler_params=GRANT,
        name="gate_sum" if squares else "gate_mix" if bases else "gate",
    )(pos, limits, *more, *shares)


def alpha_of(t_ref):
    gamma = jnp.sum(t_ref[:, 1, :])
    curvature = jnp.sum(t_ref[:, 0, :])
    return gamma / (curvature + tiny), gamma


def join_kernel(groups, pos_ref, *refs):
    me = pos_ref[0]
    ks = refs[0].shape[1]
    for p in range(groups):
        at = pl.multiple_of(share_of(me, p, groups) * ks, ks)
        for f in range(refs[p].shape[0]):
            refs[groups][f, pl.ds(at, ks), :] = refs[p][f]


def join(pos, shares, groups):
    loc, ks, wide = shares[0].shape
    return pl.pallas_call(
        lambda *refs: join_kernel(groups, *refs),
        out_shape=jax.ShapeDtypeStruct((loc, groups * ks, wide), shares[0].dtype),
        in_specs=[SMEM] + [VMEM] * groups,
        out_specs=VMEM,
        cost_estimate=cost(0, 4 * groups * shares[0].size),
        compiler_params=GRANT,
        name="join",
    )(pos, *shares)


def update_kernel(groups, pos_ref, t_ref, res_ref, foc_ref, dir_ref, *refs):
    image = refs[:groups]
    nres_ref, nfoc_ref = refs[groups:]
    alpha, _ = alpha_of(t_ref)
    me = pos_ref[0]
    loc, ks, _ = image[0].shape
    nfoc_ref[...] = foc_ref[...] + alpha * dir_ref[...]

    def body(odd):
        for p in range(groups):
            rows = pl.ds(pl.multiple_of(share_of(me, p, groups) * ks, ks), ks)
            for f in range(loc):
                for c in range(2):
                    seen = unpack(image[p][f], c, odd)
                    nres_ref[f, c, rows, :] = res_ref[f, c, rows, :] - alpha * seen

    by_parity(pos_ref, body)


def update(pos, sums, residual, focusing, direction, image, groups):
    size = residual.size
    return pl.pallas_call(
        lambda *refs: update_kernel(groups, *refs),
        out_shape=[jax.ShapeDtypeStruct(residual.shape, jnp.float32)] * 2,
        in_specs=[SMEM] + [VMEM] * (4 + groups),
        out_specs=[VMEM] * 2,
        cost_estimate=cost(4 * size, 24 * size),
        compiler_params=GRANT,
        name="update",
    )(pos, sums, residual, focusing, direction, *image)


def green_kernel(groups, pos_ref, t_ref, nfoc_ref, row_ref, *refs):
    image, kept, di, fi = [refs[i * groups : (i + 1) * groups] for i in range(4)]
    green_ref, sent_ref, corr_scr = refs[4 * groups :]
    alpha, _ = alpha_of(t_ref)
    me = pos_ref[0]
    loc, ks, _ = di[0].shape

    def body(odd):
        for p in range(groups):
            rows = pl.ds(pl.multiple_of(share_of(me, p, groups) * ks, ks), ks)
            for f in range(loc):
                row = (fi[p][f] - kept[p][f]) + alpha * (di[p][f] - image[p][f])
                for c in range(2):
                    green_ref[f, c, rows, :] = unpack(row, c, odd)

    by_parity(pos_ref, body)
    ones = jnp.ones((8, nfoc_ref.shape[3]), jnp.float32)
    dims = (((1,), (1,)), ((), ()))
    for f in range(loc):
        gr, gi, fr, fm = green_ref[f, 0], green_ref[f, 1], nfoc_ref[f, 0], nfoc_ref[f, 1]
        for c, value in enumerate((gr * fr + gi * fm, gi * fr - gr * fm)):
            line = lax.dot_general(ones, value, dims, precision=highest, preferred_element_type=jnp.float32)
            corr_scr[2 * f + c : 2 * f + c + 1, :] = line[:1]
    total = jnp.broadcast_to(row_ref[:, :HALF], (2 * loc, HALF))
    ends = jnp.concatenate([corr_scr[:, LANES:], total], axis=1)
    table = jnp.concatenate([corr_scr[:, :LANES], ends], axis=0)
    sent_ref[...] = jnp.broadcast_to(table[None], sent_ref.shape)


def green(pos, sums, new_focusing, row, image, kept, di, fi, groups):
    loc, _, k, _ = new_focusing.shape
    size = new_focusing.size
    return pl.pallas_call(
        lambda *refs: green_kernel(groups, *refs),
        out_shape=[
            jax.ShapeDtypeStruct(new_focusing.shape, jnp.float32),
            jax.ShapeDtypeStruct((sums.shape[0], 4 * loc, LANES), jnp.float32),
        ],
        in_specs=[SMEM] + [VMEM] * (3 + 4 * groups),
        out_specs=[VMEM] * 2,
        scratch_shapes=[pltpu.VMEM((2 * loc, k), jnp.float32)],
        cost_estimate=cost(12 * size, 24 * size),
        compiler_params=GRANT,
        name="green",
    )(pos, sums, new_focusing, row, *image, *kept, *di, *fi)


def turn(pos, sums, new_sums, new_gradient, direction, ranks):
    loc, _, points, n = direction.shape
    size = direction.size
    lines = 2 * loc
    scale = 1.0 / math.sqrt(n * ranks)

    def body(pos_ref, t_ref, g_ref, new_ref, dir_ref, out_ref, corr_ref):
        _, gamma = alpha_of(t_ref)
        beta = jnp.sum(g_ref[:, lines, HALF:]) / (gamma + tiny)
        out_ref[...] = new_ref[...] + beta * dir_ref[...]
        total = jnp.zeros((2 * lines, LANES), jnp.float32)
        for r in range(ranks):
            total = total + g_ref[pos_ref[0] * ranks + r]
        total = jnp.concatenate([total[:lines], total[lines:, :HALF]], axis=1) * scale
        for f in range(loc):
            corr_ref[f] = total[2 * f : 2 * f + 2]

    return pl.pallas_call(
        body,
        in_specs=[SMEM] + [VMEM] * 4,
        out_specs=[VMEM] * 2,
        out_shape=[
            jax.ShapeDtypeStruct(direction.shape, jnp.float32),
            jax.ShapeDtypeStruct((loc, 2, points), jnp.float32),
        ],
        cost_estimate=cost(2 * size, 12 * size),
        compiler_params=GRANT,
        name="turn",
    )(pos, sums, new_sums, new_gradient, direction)


def exchange(shares, groups):
    out = [shares[0]]
    for p in range(1, groups):
        pairs = [(m, share_of(m, p, groups) if groups & (groups - 1) == 0 else (p - m) % groups) for m in range(groups)]
        out.append(lax.ppermute(shares[p], "freq", pairs))
    return out


def side(deep, pick):
    pairs = []
    for z in range(deep):
        for y in range(2):
            to = pick(z, y)
            if to is not None:
                pairs.append((z * 2 + y, to[0] * 2 + to[1]))
    return pairs


def spread(own, mid):
    swap = side(4, lambda z, y: (z, 1 - y))
    near = side(4, lambda z, y: (z ^ 1, y))
    centre = side(4, lambda z, y: (3 - z, y) if z in (1, 2) else None)
    outward = side(4, lambda z, y: (0 if z == 1 else 3, y) if z in (1, 2) else None)

    def move(v, pairs):
        return lax.ppermute(v, "rcv", pairs)

    n1 = move(own, near)
    c1 = move(own, centre)
    y0 = move(own, swap)
    c2 = move(n1, centre)
    y1 = move(n1, swap)
    o1 = move(c1, outward)
    before = yield
    if before is not None:
        c2, o1, before = lax.optimization_barrier((c2, o1, before))
    yield before
    m1 = jnp.where(mid, c1, o1)
    y2 = move(m1, swap)
    o2 = move(c2, outward)
    m2 = jnp.where(mid, c2, o2)
    y3 = move(m2, swap)
    yield [own, y0, n1, y1, m1, y2, m2, y3]


def spread_all(own, mid):
    return list(spread(own, mid))[-1]


def total_over_all(sent):
    return lax.all_to_all(sent, ("freq", "rcv"), split_axis=0, concat_axis=0, tiled=True)


def per_device(reflection, starts, focusing, residual, direction, gradient):
    groups = lax.axis_size("freq")
    ranks = lax.axis_size("rcv")
    lay = lambda v: jnp.transpose(v, (0, 2, 3, 1))
    focusing, residual, direction, gradient = map(lay, (focusing, residual, direction, gradient))
    limits = jnp.transpose(starts, (1, 0))
    me = lax.axis_index("freq")
    rank = lax.axis_index("rcv")
    z, y = rank // 2, rank % 2
    mid = (z == 1) | (z == 2)
    far1 = jnp.where(z < 2, 2, 1)
    far2 = jnp.where(z < 2, 3, 0)
    pos = jnp.stack([me, y, z, z ^ 1, far1, far2]).astype(jnp.int32)

    blocks = spread_all(prep_low(pos, direction), mid)
    *res_shares, gamma_row = prep_shares(pos, residual, gradient, groups)
    res_there = exchange(res_shares, groups)
    kept_res = gate(pos, limits, res_there, groups, near=reflection)
    foc_own = prep_low(pos, focusing)
    aside = spread(foc_own, mid)
    next(aside)
    di = product(pos, reflection, blocks, groups)
    *image_there, sent = gate(pos, limits, exchange(di, groups), groups, gamma_row, groups * ranks)
    sums = total_over_all(sent)
    sums = aside.send(sums)
    foc = next(aside)
    gated_there = gate(pos, limits, image_there, groups, sums=sums, bases=kept_res)
    gated = join(pos, exchange(gated_there, groups), groups)
    blocks = spread_all(gated, mid)

    fi = product(pos, reflection, foc, groups)
    kept = gate(pos, limits, exchange(fi, groups), groups)
    kept = exchange(kept, groups)
    image = exchange(image_there, groups)
    new_residual, new_focusing = update(
        pos, sums, residual, focusing, direction, image, groups
    )
    new_gradient, row = product(pos, reflection, blocks, groups, True)
    green_field, new_sent = green(pos, sums, new_focusing, row, image, kept, di, fi, groups)
    new_sums = total_over_all(new_sent)
    new_direction, focal_correlation = turn(pos, sums, new_sums, new_gradient, direction, ranks)
    back = lambda v: jnp.transpose(v, (0, 3, 1, 2))
    return (back(new_focusing), back(new_residual), back(new_direction), back(green_field), focal_correlation)


def chosen(mesh):
    def run(reflection, starts, *fields):
        rows, points = starts.shape
        suits = (
            mesh.shape["rcv"] == 8
            and rows % LANES == HALF
            and rows > LANES
            and points % (16 * mesh.shape["freq"]) == 0
            and points == LANES + HALF
        )
        plan = per_device if suits else per_device_general
        return plan(reflection, starts, *fields)

    return run


def solution(mesh):
    return jax.shard_map(
        chosen(mesh),
        mesh=mesh,
        in_specs=(
            P("freq", None, "rcv", None),
            P("rcv", None),
            P("freq", "rcv", None, None),
            P("freq", "rcv", None, None),
            P("freq", "rcv", None, None),
            P("freq", "rcv", None, None),
        ),
        out_specs=(
            P("freq", "rcv", None, None),
            P("freq", "rcv", None, None),
            P("freq", "rcv", None, None),
            P("freq", "rcv", None, None),
            P("freq", None, None),
        ),
        check_vma=False,
    )
```
